512 devices in a mesh: grp: 16 (over y, core), dev: 32 (over x, z).
Axes of the slice: x: 4, y: 8, z: 8, core: 2. Of those that a mesh axis runs over, the one named last changes fastest.
Arguments:
- memory: float32 [262144, 256], P(('grp', 'dev')), may hold values from -4 to 4
- want_end: int32 [512, 512, 2], P(('grp', 'dev')), may hold values from -1 to 511, as said below
- want_near: int32 [512, 512, 16], P(('grp', 'dev')), may hold values from -1 to 511, as said below
- end_slot: int32 [65536, 2], P(('grp', 'dev')), may hold values from 0 to 1023, as said below
- near_slot: int32 [65536, 20], P(('grp', 'dev')), may hold values from 0 to 8191, as said below
- near_count: int32 [65536, 2], P(('grp', 'dev')), may hold values from 1 to 10
- event_time: int32 [65536], P(('grp', 'dev')), may hold values from 1024 to 131071
- near_time: int32 [65536, 20], P(('grp', 'dev')), may hold values from 1 to 131071, as said below
- frequency: float32 [128], replicated, may hold values from 0.001 to 0.5
- phases: float32 [128], replicated, may hold values from -3.140625 to 3.140625
- query_weight: bfloat16 [384, 256], replicated, may hold values from -0.3125 to 0.3125
- key_weight: bfloat16 [384, 256], replicated, may hold values from -0.3125 to 0.3125
- value_weight: bfloat16 [384, 256], replicated, may hold values from -0.3125 to 0.3125
- out_weight: bfloat16 [512, 256], replicated, may hold values from -0.25 to 0.25
- out_bias: float32 [256], replicated, may hold values from -4 to 4
- message_in: bfloat16 [512, 256], replicated, may hold values from -0.25 to 0.25
- message_out: bfloat16 [256, 256], replicated, may hold values from -0.375 to 0.375
- input_weight: bfloat16 [256, 768], replicated, may hold values from -0.375 to 0.375
- state_weight: bfloat16 [256, 768], replicated, may hold values from -0.375 to 0.375
- update_bias: float32 [768], replicated, may hold values from -4 to 4
Outputs:
- new_memory: float32 [262144, 256], P(('grp', 'dev'))
- event_embed: bfloat16 [65536, 512], P(('grp', 'dev'))
The draws below stay inside these ranges and needn't reach their ends.
Inputs may be any that keep to these rules, and one draw needn't show every extreme that they name: `want_end`: for each asking device a quarter of the owners get 2 filled slots, half get 1, a quarter none, chosen by the draw; filled slots come first and hold a row of the owner's 512 rows, empty slots hold -1. `want_near`: all devices of one grp index ask each owner for the same slots. 64 owners, the same for every asking device, get all 16 slots filled; every other owner gets 16 // 2 to 15 filled slots; filled slots come first and hold a row of the owner's rows, empty slots hold -1. `end_slot`: the value o * 2 + s names slot s of owner o in the event's own device's want_end, always a filled slot. `near_slot`: the value o * 16 + s names slot s of owner o in the event's own device's want_near, always a filled slot. near_time[e, i] lies in event_time[e] - 1023 to event_time[e].
All inputs are finite; a program needn't handle non-finite values.
Results may differ from the reference program's by a relative error of at most 0.0042.
Values may be sent and summed in bfloat16 or wider, within the bound.
No kernel may reach another device: no remote copies, remote signals or barrier semaphores. Data moves between devices by JAX's collectives and lax.ppermute only.
A program may use at most 64 MiB of HBM per device.

```python
import math
import jax
import jax.numpy as jnp
from jax import lax

W = 256
TD = 128
HEADS = 2
K = 10
CAP_E = 2
CAP_N = 16
WINDOW = 1024
EV_DEV = 128
NODES_DEV = 512
OWNERS = 512
HOT = 64
EVENTS = 65536
NODES = 262144
N_GRP = 16


def owner_ranking(key):
    key_list = jax.random.split(key, OWNERS)
    shuffles = jax.vmap(lambda single: jax.random.permutation(single, OWNERS))(key_list)
    return jnp.argsort(shuffles, axis=1, stable=True)


def end_layout(key):
    folded = jax.random.fold_in(key, 101)
    key_order, key_rows = jax.random.split(folded)
    ranking = owner_ranking(key_order)
    filled_count = jnp.where(ranking < OWNERS // 4, 2, jnp.where(ranking < 3 * (OWNERS // 4), 1, 0))
    filled = jnp.arange(CAP_E)[None, None, :] < filled_count[:, :, None]
    picked = jax.random.randint(key_rows, (OWNERS, OWNERS, CAP_E), 0, NODES_DEV)
    return (jnp.where(filled, picked, -1).astype(jnp.int32), filled)


def near_layout(key):
    folded = jax.random.fold_in(key, 201)
    key_hot, key_count, key_rows = jax.random.split(folded, 3)
    members = OWNERS // N_GRP
    hot_rank = jnp.argsort(jax.random.permutation(key_hot, OWNERS), stable=True)
    group_count = jax.random.randint(key_count, (N_GRP, OWNERS), CAP_N // 2, CAP_N)
    group_count = jnp.where(hot_rank[None, :] < HOT, CAP_N, group_count)
    group_rows = jax.random.randint(key_rows, (N_GRP, OWNERS, CAP_N), 0, NODES_DEV)
    filled_count = jnp.repeat(group_count, members, axis=0)
    picked = jnp.repeat(group_rows, members, axis=0)
    filled = jnp.arange(CAP_N)[None, None, :] < filled_count[:, :, None]
    return (jnp.where(filled, picked, -1).astype(jnp.int32), filled, filled_count)


def time_layout(key):
    folded = jax.random.fold_in(key, 301)
    key_event, key_age = jax.random.split(folded)
    stamps = jax.random.randint(key_event, (EVENTS,), WINDOW, 2 ** 17)
    ages = jax.random.randint(key_age, (EVENTS, 2 * K), 0, WINDOW)
    return (stamps.astype(jnp.int32), (stamps[:, None] - ages).astype(jnp.int32))


def draw_want_end(key, part):
    return end_layout(key)[0]


def draw_want_near(key, part):
    return near_layout(key)[0]


def draw_end_slot(key, part):
    wanted, filled = end_layout(key)
    flattened = filled.reshape(OWNERS, OWNERS * CAP_E)
    ordering = jnp.argsort(jnp.where(flattened, 0, 1), axis=1, stable=True)
    chosen = jax.random.randint(jax.random.fold_in(key, 102), (OWNERS, 2 * EV_DEV), 0, OWNERS)
    return jnp.take_along_axis(ordering, chosen, axis=1).reshape(EVENTS, 2).astype(jnp.int32)


def draw_near_slot(key, part):
    wanted, filled, filled_count = near_layout(key)
    flattened = filled.reshape(OWNERS, OWNERS * CAP_N)
    ordering = jnp.argsort(jnp.where(flattened, 0, 1), axis=1, stable=True)
    totals = jnp.sum(filled_count, axis=1)
    chosen = jax.random.randint(jax.random.fold_in(key, 202), (OWNERS, 2 * K * EV_DEV), 0, 2 ** 30) % totals[:, None]
    return jnp.take_along_axis(ordering, chosen, axis=1).reshape(EVENTS, 2 * K).astype(jnp.int32)


def draw_event_time(key, part):
    return time_layout(key)[0]


def draw_near_time(key, part):
    return time_layout(key)[1]


def touch_ends(drawn, own_key, low, high):
    extent = drawn.shape
    spot = [jax.random.randint(jax.random.fold_in(own_key, axis), (), 0, extent[axis]) for axis in range(len(extent))]
    drawn = drawn.at[tuple(spot)].set(low)
    longest = extent.index(max(extent))
    spot[longest] = (spot[longest] + 1) % extent[longest]
    return drawn.at[tuple(spot)].set(high)


def steps_of(key, extent, cuts, smallest, high):
    loudness, own = 1.0, jax.random.fold_in(key, 6)
    for dim, parts in cuts:
        draws = jnp.exp(jax.random.uniform(jax.random.fold_in(own, dim), (parts,), jnp.float32, smallest / len(cuts), high / len(cuts)))
        loudness = loudness * jnp.repeat(draws, extent[dim] // parts).reshape([-1 if axis == dim else 1 for axis in range(len(extent))])
    return loudness


def bell_draw(key, dims, spread, most, cuts=(), held_as=jnp.bfloat16):
    array = spread * jax.random.normal(key, dims, jnp.float32)
    if cuts:
        array = array * steps_of(key, dims, cuts, -0.22, 0.18)
    return jnp.clip(array, -most, most).astype(held_as)


def setup_inputs(seed: int = 0) -> dict:
    splits = jax.random.split(jax.random.key(seed), 21)
    memory = bell_draw(splits[0], (NODES, W), 1.0, 4.0, ((0, 512),), jnp.float32)
    want_end = draw_want_end(jax.random.fold_in(splits[20], 71), 0)
    want_near = draw_want_near(jax.random.fold_in(splits[20], 71), 0)
    end_slot = draw_end_slot(jax.random.fold_in(splits[20], 71), 0)
    near_slot = draw_near_slot(jax.random.fold_in(splits[20], 71), 0)
    near_count = touch_ends(jax.random.randint(splits[5], (EVENTS, 2), 1, K + 1), jax.random.fold_in(splits[5], 1), 1, K).astype(jnp.int32)
    event_time = draw_event_time(jax.random.fold_in(splits[20], 71), 0)
    near_time = draw_near_time(jax.random.fold_in(splits[20], 71), 0)
    frequency = jnp.clip(jnp.exp(jax.random.uniform(splits[8], (TD,), jnp.float32, math.log(0.001), math.log(0.5))), 0.001, 0.5)
    phases = jnp.clip(jax.random.uniform(splits[9], (TD,), jnp.float32, -3.140625, 3.140625), -3.140625, 3.140625)
    query_weight = bell_draw(splits[10], (W + TD, W), (W + TD) ** -0.5, 0.3125)
    key_weight = bell_draw(splits[11], (W + TD, W), (W + TD) ** -0.5, 0.3125)
    value_weight = bell_draw(splits[12], (W + TD, W), (W + TD) ** -0.5, 0.3125)
    out_weight = bell_draw(splits[13], (2 * W, W), (2 * W) ** -0.5, 0.25)
    out_bias = bell_draw(splits[14], (W,), 1.0, 4.0, (), jnp.float32)
    message_in = bell_draw(splits[15], (2 * W, W), (2 * W) ** -0.5, 0.25)
    message_out = bell_draw(splits[16], (W, W), W ** -0.5, 0.375)
    input_weight = bell_draw(splits[17], (W, 3 * W), W ** -0.5, 0.375)
    state_weight = bell_draw(splits[18], (W, 3 * W), W ** -0.5, 0.375)
    update_bias = bell_draw(splits[19], (3 * W,), 1.0, 4.0, (), jnp.float32)
    return dict(memory=memory, want_end=want_end, want_near=want_near, end_slot=end_slot, near_slot=near_slot, near_count=near_count, event_time=event_time, near_time=near_time, frequency=frequency, phases=phases, query_weight=query_weight, key_weight=key_weight, value_weight=value_weight, out_weight=out_weight, out_bias=out_bias, message_in=message_in, message_out=message_out, input_weight=input_weight, state_weight=state_weight, update_bias=update_bias)


def event_block(end_rows, near_rows, elapsed, near_count, frequency, phases, query_weight, key_weight, value_weight, out_weight, out_bias, message_in, message_out):
    highest = lax.Precision.HIGHEST
    events = end_rows.shape[0]
    row_width = end_rows.shape[-1]
    head_size = row_width // HEADS
    fixed_code = jnp.broadcast_to(jnp.cos(phases).astype(jnp.bfloat16), (events, 2, phases.shape[0]))
    near_code = jnp.cos(elapsed[..., None] * frequency + phases).astype(jnp.bfloat16)
    query_in = jnp.concatenate([end_rows, fixed_code], -1).astype(jnp.float32)
    queries = jnp.einsum('ejc,cd->ejd', query_in, query_weight.astype(jnp.float32), precision=highest)
    near_in = jnp.concatenate([near_rows, near_code], -1).astype(jnp.float32)
    key_rows = jnp.einsum('eic,cd->eid', near_in, key_weight.astype(jnp.float32), precision=highest)
    values = jnp.einsum('eic,cd->eid', near_in, value_weight.astype(jnp.float32), precision=highest)
    queries = queries.reshape(events, 2, HEADS, head_size)
    key_rows = key_rows.reshape(events, 2, K, HEADS, head_size)
    values = values.reshape(events, 2, K, HEADS, head_size)
    scores = jnp.einsum('ejhc,ejkhc->ejhk', queries, key_rows, precision=highest) / math.sqrt(head_size)
    usable = jnp.arange(K)[None, None, None, :] < near_count[:, :, None, None]
    exponent = jnp.where(usable, jnp.exp(scores), jnp.zeros_like(scores))
    weight = exponent / lax.optimization_barrier(jnp.sum(exponent, axis=-1, keepdims=True))
    attended = jnp.einsum('ejhk,ejkhc->ejhc', weight, values, precision=highest).reshape(events, 2, row_width).astype(jnp.bfloat16)
    joined = jnp.concatenate([attended, end_rows], -1).astype(jnp.float32)
    embedded = jax.nn.relu(jnp.einsum('ejc,cd->ejd', joined, out_weight.astype(jnp.float32), precision=highest) + out_bias).astype(jnp.bfloat16)
    paired = jnp.concatenate([embedded, embedded[:, ::-1]], -1).astype(jnp.float32)
    hidden = jax.nn.relu(jnp.einsum('ejc,cd->ejd', paired, message_in.astype(jnp.float32), precision=highest)).astype(jnp.bfloat16)
    message = jnp.einsum('ejc,cd->ejd', hidden.astype(jnp.float32), message_out.astype(jnp.float32), precision=highest)
    return (embedded, message)

def gru_update(memory, totals, counts, input_weight, state_weight, update_bias):
    row_width = memory.shape[1]
    mem_half = memory.astype(jnp.bfloat16)
    averaged = (totals / jnp.maximum(counts, 1.0)[:, None]).astype(jnp.bfloat16)
    from_msg = jnp.dot(averaged, input_weight, preferred_element_type=jnp.float32)
    from_state = jnp.dot(mem_half, state_weight, preferred_element_type=jnp.float32)
    update_gate = jax.nn.sigmoid(from_msg[:, :row_width] + from_state[:, :row_width] + update_bias[:row_width])
    reset_gate = jax.nn.sigmoid(from_msg[:, row_width:2 * row_width] + from_state[:, row_width:2 * row_width] + update_bias[row_width:2 * row_width])
    candidate = jnp.tanh(from_msg[:, 2 * row_width:] + update_bias[2 * row_width:] + reset_gate * from_state[:, 2 * row_width:])
    updated = (1.0 - update_gate) * candidate + update_gate * memory
    return jnp.where((counts > 0)[:, None], updated, memory)

def reference(memory, want_end, want_near, end_slot, near_slot, near_count, event_time, near_time, frequency, phases, query_weight, key_weight, value_weight, out_weight, out_bias, message_in, message_out, input_weight, state_weight, update_bias):
    mem_half = memory.astype(jnp.bfloat16)
    row_width = memory.shape[1]
    flat_end = want_end.reshape(OWNERS, OWNERS * CAP_E)
    flat_near = want_near.reshape(OWNERS, OWNERS * CAP_N)

    def per_device(device):
        offset = (device * EV_DEV).astype(jnp.int32)
        slots_end = lax.dynamic_slice_in_dim(end_slot, offset, EV_DEV, 0)
        slots_near = lax.dynamic_slice_in_dim(near_slot, offset, EV_DEV, 0)
        counts_near = lax.dynamic_slice_in_dim(near_count, offset, EV_DEV, 0)
        stamps = lax.dynamic_slice_in_dim(event_time, offset, EV_DEV, 0)
        near_stamps = lax.dynamic_slice_in_dim(near_time, offset, EV_DEV, 0)
        local_end = lax.dynamic_index_in_dim(flat_end, device, 0, keepdims=False)[slots_end]
        local_near = lax.dynamic_index_in_dim(flat_near, device, 0, keepdims=False)[slots_near]
        end_node = (slots_end // CAP_E * NODES_DEV + local_end).astype(jnp.int32)
        near_node = (slots_near // CAP_N * NODES_DEV + local_near).astype(jnp.int32)
        elapsed = (stamps[:, None] - near_stamps).astype(jnp.float32)
        embedded, message = event_block(mem_half[end_node], mem_half[near_node], elapsed, counts_near, frequency, phases, query_weight, key_weight, value_weight, out_weight, out_bias, message_in, message_out)
        return (embedded, message, end_node)
    embedded, message, end_node = lax.map(per_device, jnp.arange(OWNERS, dtype=jnp.int32))
    flat_nodes = end_node.reshape(-1)
    totals = jnp.zeros((NODES, row_width), jnp.float32).at[flat_nodes].add(message.reshape(-1, row_width))
    counts = jnp.zeros((NODES,), jnp.float32).at[flat_nodes].add(jnp.ones(flat_nodes.shape, jnp.float32))

    def per_owner(blocks):
        return gru_update(blocks[0], blocks[1], blocks[2], input_weight, state_weight, update_bias)
    new_memory = lax.map(per_owner, (memory.reshape(OWNERS, NODES_DEV, row_width), totals.reshape(OWNERS, NODES_DEV, row_width), counts.reshape(OWNERS, NODES_DEV))).reshape(NODES, row_width)
    return (new_memory, embedded.reshape(EVENTS, 2 * row_width))
```

```python
import math

import jax
import jax.numpy as jnp
from jax import lax
from jax.sharding import PartitionSpec as P

HEADS = 2
K = 10
CAP_E = 2
CAP_N = 16
CAP = 72
LANES = 128
SHIFT = 65536


def hot(index, size, axis):
    index = jnp.expand_dims(index, axis)
    grid = lax.broadcasted_iota(jnp.int32, index.shape[:axis] + (size,) + index.shape[axis + 1 :], axis)
    return (index == grid).astype(jnp.bfloat16)


def pick(index, table):
    return jnp.dot(hot(index, table.shape[0], 1), table, preferred_element_type=jnp.float32).astype(
        jnp.bfloat16
    )


def exchange(x, axis):
    return lax.all_to_all(x, axis, split_axis=0, concat_axis=0, tiled=True)


def event_block(
    end_rows,
    near_rows,
    elapsed,
    near_count,
    frequency,
    phases,
    query_weight,
    key_weight,
    value_weight,
    out_weight,
    out_bias,
    message_in,
    message_out,
):
    events = end_rows.shape[1]
    row_width = end_rows.shape[-1]
    head_size = row_width // HEADS
    fixed_code = jnp.broadcast_to(
        jnp.cos(phases).astype(jnp.bfloat16), (2, events, phases.shape[0])
    )
    near_code = jnp.cos(elapsed[..., None] * frequency + phases).astype(jnp.bfloat16)
    query_in = jnp.concatenate([end_rows, fixed_code], -1)
    queries = jnp.einsum("jec,cd->jed", query_in, query_weight, preferred_element_type=jnp.float32)
    near_in = jnp.concatenate([near_rows, near_code], -1)
    key_rows = jnp.einsum("jkec,cd->jked", near_in, key_weight, preferred_element_type=jnp.float32)
    values = jnp.einsum("jkec,cd->jked", near_in, value_weight, preferred_element_type=jnp.float32)
    usable = jnp.arange(K)[None, :, None] < near_count[:, None, :]
    pieces = []
    for head in range(HEADS):
        low = head * head_size
        high = low + head_size
        scores = jnp.sum(
            queries[:, None, :, low:high] * key_rows[..., low:high], axis=-1
        ) / math.sqrt(head_size)
        exponent = jnp.where(usable, jnp.exp(scores), jnp.zeros_like(scores))
        weight = exponent / jnp.sum(exponent, axis=1, keepdims=True)
        pieces.append(jnp.sum(weight[..., None] * values[..., low:high], axis=1))
    attended = jnp.concatenate(pieces, -1).astype(jnp.bfloat16)
    joined = jnp.concatenate([attended, end_rows], -1)
    embedded = jax.nn.relu(
        jnp.einsum("jec,cd->jed", joined, out_weight, preferred_element_type=jnp.float32) + out_bias
    ).astype(jnp.bfloat16)
    paired = jnp.concatenate([embedded, embedded[::-1]], -1)
    hidden = jax.nn.relu(
        jnp.einsum("jec,cd->jed", paired, message_in, preferred_element_type=jnp.float32)
    ).astype(jnp.bfloat16)
    message = jnp.einsum("jec,cd->jed", hidden, message_out, preferred_element_type=jnp.float32)
    return (embedded, message)


def gru_update(memory, mem_half, totals, counts, input_weight, state_weight, update_bias):
    row_width = memory.shape[1]
    averaged = (totals / jnp.maximum(counts, 1.0)[:, None]).astype(jnp.bfloat16)
    from_msg = jnp.dot(averaged, input_weight, preferred_element_type=jnp.float32)
    from_state = jnp.dot(mem_half, state_weight, preferred_element_type=jnp.float32)
    update_gate = jax.nn.sigmoid(
        from_msg[:, :row_width] + from_state[:, :row_width] + update_bias[:row_width]
    )
    reset_gate = jax.nn.sigmoid(
        from_msg[:, row_width : 2 * row_width]
        + from_state[:, row_width : 2 * row_width]
        + update_bias[row_width : 2 * row_width]
    )
    candidate = jnp.tanh(
        from_msg[:, 2 * row_width :]
        + update_bias[2 * row_width :]
        + reset_gate * from_state[:, 2 * row_width :]
    )
    updated = (1.0 - update_gate) * candidate + update_gate * memory
    return jnp.where((counts > 0)[:, None], updated, memory)


def local(
    memory,
    want_end,
    want_near,
    end_slot,
    near_slot,
    near_count,
    event_time,
    near_time,
    frequency,
    phases,
    query_weight,
    key_weight,
    value_weight,
    out_weight,
    out_bias,
    message_in,
    message_out,
    input_weight,
    state_weight,
    update_bias,
):
    groups = lax.axis_size("grp")
    members = lax.axis_size("dev")
    nodes, row_width = memory.shape
    events = end_slot.shape[0]
    block = groups * CAP_N
    mem_half = memory.astype(jnp.bfloat16)
    counted = jnp.transpose(near_count)

    near_value = jnp.transpose(near_slot).reshape(-1)
    owner = near_value // CAP_N
    member = owner % members
    place = (owner // members) * CAP_N + near_value % CAP_N
    usable = (jnp.arange(K)[None, :, None] < counted[:, None, :]).reshape(-1)
    member_hot = hot(jnp.where(usable, member, -1), members, 0)
    place_hot = hot(place, block, 0)
    used = (
        lax.dot_general(
            member_hot, place_hot, (((1,), (1,)), ((), ())), preferred_element_type=jnp.float32
        )
        > 0
    )
    before = (jnp.arange(block)[:, None] < jnp.arange(block)[None, :]).astype(jnp.bfloat16)
    rank = jnp.dot(used.astype(jnp.bfloat16), before, preferred_element_type=jnp.float32)
    most = jnp.max(jnp.sum(used.astype(jnp.int32), axis=1))
    rank_or_none = jnp.where(used, rank.astype(jnp.int32), -1)
    listed = jnp.sum(
        jnp.where(
            rank_or_none[:, None, :] == jnp.arange(CAP)[None, :, None],
            jnp.arange(block)[None, None, :],
            0,
        ),
        axis=2,
    )
    ref_rank = jnp.sum(
        jnp.dot(rank.astype(jnp.bfloat16), place_hot, preferred_element_type=jnp.float32)
        * member_hot.astype(jnp.float32),
        axis=0,
    ).astype(jnp.int32)

    end_value = jnp.transpose(end_slot).reshape(-1)
    end_hot = hot(end_value, groups * members * CAP_E, 0)
    slot_count = jnp.sum(end_hot.astype(jnp.float32), axis=1).astype(jnp.int32)
    wanted = want_end.reshape(-1)
    asked = jnp.where(wanted >= 0, wanted + SHIFT * slot_count, -1).reshape(groups, members * CAP_E)

    mine = lax.axis_index("dev")
    ask_near = lax.dynamic_index_in_dim(
        want_near.reshape(groups, members, CAP_N), mine, 1, keepdims=False
    )
    first = jnp.concatenate(
        [
            asked,
            ask_near,
            jnp.broadcast_to(most, (groups, LANES - members * CAP_E - CAP_N)),
        ],
        1,
    )
    first = exchange(first, "grp")
    got_near = first[:, members * CAP_E : members * CAP_E + CAP_N]
    most = jnp.max(first[:, members * CAP_E + CAP_N :])
    passed = jnp.transpose(
        first[:, : members * CAP_E].reshape(groups, members, CAP_E), (1, 0, 2)
    ).reshape(members, groups * CAP_E)
    second = jnp.concatenate(
        [
            passed,
            listed,
            jnp.broadcast_to(most, (members, LANES - groups * CAP_E - CAP)),
        ],
        1,
    )
    second = exchange(second, "dev")
    got_listed = second[:, groups * CAP_E : groups * CAP_E + CAP]
    most = jnp.max(second[:, groups * CAP_E + CAP :])
    got_code = second[:, : groups * CAP_E].reshape(members, groups, CAP_E)
    got_code = jnp.transpose(got_code, (1, 0, 2)).reshape(groups, members * CAP_E)
    got_end = jnp.where(got_code >= 0, got_code % SHIFT, -1)
    got_count = jnp.where(got_code >= 0, got_code // SHIFT, 0)

    row_index = jnp.concatenate([got_near, got_end], 1).reshape(-1)
    rows = exchange(pick(row_index, mem_half).reshape(groups, -1, row_width), "grp")
    near_block = rows[:, :CAP_N].reshape(block, row_width)
    end_part = jnp.transpose(
        rows[:, CAP_N:].reshape(groups, members, CAP_E, row_width), (1, 0, 2, 3)
    ).reshape(members, groups * CAP_E, row_width)
    near_part = pick(got_listed.reshape(-1), near_block).reshape(members, CAP, row_width)
    table = exchange(jnp.concatenate([near_part, end_part], 1), "dev")
    per_member = CAP + groups * CAP_E
    table = table.reshape(members * per_member, row_width)

    end_owner = end_value // CAP_E
    end_index = (
        (end_owner % members) * per_member
        + CAP
        + (end_owner // members) * CAP_E
        + end_value % CAP_E
    )
    near_index = jnp.where(usable, member * per_member + ref_rank, 0)
    fetched = jnp.take(
        table, jnp.concatenate([near_index, end_index]), axis=0, mode="clip"
    )
    end_rows = fetched[2 * K * events :].reshape(2, events, row_width)

    def whole():
        full = exchange(jnp.broadcast_to(near_block[None], (members, block, row_width)), "dev")
        return jnp.take(
            full.reshape(members * block, row_width), member * block + place, axis=0, mode="clip"
        )

    near_rows = lax.cond(most > CAP, whole, lambda: fetched[: 2 * K * events])
    near_rows = near_rows.reshape(2, K, events, row_width)
    elapsed = (
        (event_time[None, :] - jnp.transpose(near_time)).astype(jnp.float32).reshape(2, K, events)
    )
    embedded, message = event_block(
        end_rows,
        near_rows,
        elapsed,
        counted,
        frequency,
        phases,
        query_weight,
        key_weight,
        value_weight,
        out_weight,
        out_bias,
        message_in,
        message_out,
    )
    message = message.reshape(-1, row_width)
    message_high = lax.reduce_precision(message, 8, 7)
    slot_sum = jnp.dot(
        end_hot, message_high.astype(jnp.bfloat16), preferred_element_type=jnp.float32
    ) + jnp.dot(
        end_hot, (message - message_high).astype(jnp.bfloat16), preferred_element_type=jnp.float32
    )
    news = exchange(
        slot_sum.astype(jnp.bfloat16).reshape(groups * members, CAP_E * row_width), ("grp", "dev")
    ).reshape(-1, row_width)
    owned = got_end.reshape(-1)
    owned_hot = hot(owned, nodes, 0)
    totals = jnp.dot(owned_hot, news, preferred_element_type=jnp.float32)
    counts = jnp.sum(
        jnp.where(
            owned[None, :] == jnp.arange(nodes)[:, None], got_count.reshape(1, -1), 0
        ),
        axis=1,
    ).astype(jnp.float32)
    new_memory = gru_update(
        memory, mem_half, totals, counts, input_weight, state_weight, update_bias
    )
    return (new_memory, jnp.concatenate([embedded[0], embedded[1]], 1))


def solution(mesh):
    in_specs = (
        P(("grp", "dev"), None),
        P(("grp", "dev"), None, None),
        P(("grp", "dev"), None, None),
        P(("grp", "dev"), None),
        P(("grp", "dev"), None),
        P(("grp", "dev"), None),
        P(("grp", "dev")),
        P(("grp", "dev"), None),
        P(),
        P(),
        P(),
        P(),
        P(),
        P(),
        P(),
        P(),
        P(),
        P(),
        P(),
        P(),
    )
    out_specs = (P(("grp", "dev"), None), P(("grp", "dev"), None))
    return jax.shard_map(local, mesh=mesh, in_specs=in_specs, out_specs=out_specs, check_vma=False)
```

```python
import math

import jax
import jax.numpy as jnp
from jax import lax
from jax.sharding import PartitionSpec as P

HEADS = 2
K = 10
CAP_E = 2
CAP_N = 16
CAP = 88
LANES = 128
SHIFT = 65536


def hot(index, size, axis):
    index = jnp.expand_dims(index, axis)
    grid = lax.broadcasted_iota(jnp.int32, index.shape[:axis] + (size,) + index.shape[axis + 1 :], axis)
    return (index == grid).astype(jnp.bfloat16)


def pick(index, table):
    return jnp.dot(hot(index, table.shape[0], 1), table, preferred_element_type=jnp.float32).astype(
        jnp.bfloat16
    )


def split_slot(value, members, slots):
    width = slots.bit_length() - 1
    owner = value >> width
    return owner & (members - 1), ((owner >> (members.bit_length() - 1)) << width) | (value & (slots - 1))


def exchange(x, axis):
    return lax.all_to_all(x, axis, split_axis=0, concat_axis=0, tiled=True)


def event_block(
    end_rows,
    near_rows,
    elapsed,
    near_count,
    frequency,
    phases,
    query_weight,
    key_weight,
    value_weight,
    out_weight,
    out_bias,
    message_in,
    message_out,
):
    events = end_rows.shape[1]
    row_width = end_rows.shape[-1]
    head_size = row_width // HEADS
    fixed_code = jnp.broadcast_to(
        jnp.cos(phases).astype(jnp.bfloat16), (2, events, phases.shape[0])
    )
    near_code = jnp.cos(elapsed[..., None] * frequency + phases).astype(jnp.bfloat16)
    query_in = jnp.concatenate([end_rows, fixed_code], -1)
    queries = jnp.einsum("jec,cd->jed", query_in, query_weight, preferred_element_type=jnp.float32)
    near_in = jnp.concatenate([near_rows, near_code], -1)
    key_rows = jnp.einsum("jkec,cd->jked", near_in, key_weight, preferred_element_type=jnp.float32)
    values = jnp.einsum("jkec,cd->jked", near_in, value_weight, preferred_element_type=jnp.float32)
    usable = jnp.arange(K)[None, :, None] < near_count[:, None, :]
    pieces = []
    for head in range(HEADS):
        low = head * head_size
        high = low + head_size
        scores = jnp.sum(
            queries[:, None, :, low:high] * key_rows[..., low:high], axis=-1
        ) / math.sqrt(head_size)
        exponent = jnp.where(usable, jnp.exp(scores), jnp.zeros_like(scores))
        weight = exponent / jnp.sum(exponent, axis=1, keepdims=True)
        pieces.append(jnp.sum(weight[..., None] * values[..., low:high], axis=1))
    attended = jnp.concatenate(pieces, -1).astype(jnp.bfloat16)
    joined = jnp.concatenate([attended, end_rows], -1)
    embedded = jax.nn.relu(
        jnp.einsum("jec,cd->jed", joined, out_weight, preferred_element_type=jnp.float32) + out_bias
    ).astype(jnp.bfloat16)
    paired = jnp.concatenate([embedded, embedded[::-1]], -1)
    hidden = jax.nn.relu(
        jnp.einsum("jec,cd->jed", paired, message_in, preferred_element_type=jnp.float32)
    ).astype(jnp.bfloat16)
    message = jnp.einsum("jec,cd->jed", hidden, message_out, preferred_element_type=jnp.float32)
    return (embedded, message)


def gru_update(memory, mem_half, totals, counts, input_weight, state_weight, update_bias):
    row_width = memory.shape[1]
    averaged = (totals / jnp.maximum(counts, 1.0)[:, None]).astype(jnp.bfloat16)
    from_msg = jnp.dot(averaged, input_weight, preferred_element_type=jnp.float32)
    from_state = jnp.dot(mem_half, state_weight, preferred_element_type=jnp.float32)
    update_gate = jax.nn.sigmoid(
        from_msg[:, :row_width] + from_state[:, :row_width] + update_bias[:row_width]
    )
    reset_gate = jax.nn.sigmoid(
        from_msg[:, row_width : 2 * row_width]
        + from_state[:, row_width : 2 * row_width]
        + update_bias[row_width : 2 * row_width]
    )
    candidate = jnp.tanh(
        from_msg[:, 2 * row_width :]
        + update_bias[2 * row_width :]
        + reset_gate * from_state[:, 2 * row_width :]
    )
    updated = (1.0 - update_gate) * candidate + update_gate * memory
    return jnp.where((counts > 0)[:, None], updated, memory)


def local(
    memory,
    want_end,
    want_near,
    end_slot,
    near_slot,
    near_count,
    event_time,
    near_time,
    frequency,
    phases,
    query_weight,
    key_weight,
    value_weight,
    out_weight,
    out_bias,
    message_in,
    message_out,
    input_weight,
    state_weight,
    update_bias,
):
    groups = lax.axis_size("grp")
    members = lax.axis_size("dev")
    nodes, row_width = memory.shape
    events = end_slot.shape[0]
    block = groups * CAP_N
    ends = groups * CAP_E
    places = block + ends
    mem_half = memory.astype(jnp.bfloat16)
    counted = jnp.transpose(near_count)

    near_value = jnp.transpose(near_slot).reshape(-1)
    end_value = jnp.transpose(end_slot).reshape(-1)
    near_member, near_place = split_slot(near_value, members, CAP_N)
    end_member, end_place = split_slot(end_value, members, CAP_E)
    usable = (jnp.arange(K)[None, :, None] < counted[:, None, :]).reshape(-1)
    member = jnp.concatenate([jnp.where(usable, near_member, -1), end_member])
    place = jnp.concatenate([near_place, end_place + block])
    member_hot = hot(member, members, 0)
    place_hot = hot(place, places, 0)
    used = (
        lax.dot_general(
            member_hot, place_hot, (((1,), (1,)), ((), ())), preferred_element_type=jnp.float32
        )
        > 0
    )
    before = (jnp.arange(places)[:, None] < jnp.arange(places)[None, :]).astype(jnp.bfloat16)
    rank = jnp.dot(used.astype(jnp.bfloat16), before, preferred_element_type=jnp.float32)
    most = jnp.max(jnp.sum(used.astype(jnp.int32), axis=1))
    rank_or_none = jnp.where(used, rank.astype(jnp.int32), -1)
    listed = jnp.sum(
        jnp.where(
            rank_or_none[:, None, :] == jnp.arange(CAP)[None, :, None],
            jnp.arange(places)[None, None, :],
            0,
        ),
        axis=2,
    )
    ref_rank = jnp.sum(
        jnp.dot(rank.astype(jnp.bfloat16), place_hot, preferred_element_type=jnp.float32)
        * member_hot.astype(jnp.float32),
        axis=0,
    ).astype(jnp.int32)
    index = jnp.where(member >= 0, member * CAP + jnp.minimum(ref_rank, CAP - 1), 0)

    end_hot = hot(end_value, groups * members * CAP_E, 0)
    slot_count = jnp.sum(end_hot.astype(jnp.float32), axis=1).astype(jnp.int32)
    wanted = want_end.reshape(-1)
    asked = jnp.where(wanted >= 0, wanted + SHIFT * slot_count, -1).reshape(groups, members * CAP_E)

    mine = lax.axis_index("dev")
    ask_near = lax.dynamic_index_in_dim(
        want_near.reshape(groups, members, CAP_N), mine, 1, keepdims=False
    )
    first = jnp.concatenate(
        [
            asked,
            ask_near,
            jnp.broadcast_to(most, (groups, LANES - members * CAP_E - CAP_N)),
        ],
        1,
    )
    first = exchange(first, "grp")
    got_near = first[:, members * CAP_E : members * CAP_E + CAP_N]
    most = jnp.max(first[:, members * CAP_E + CAP_N :])
    passed = jnp.transpose(
        first[:, : members * CAP_E].reshape(groups, members, CAP_E), (1, 0, 2)
    ).reshape(members, ends)
    second = jnp.concatenate(
        [
            passed,
            listed,
            jnp.broadcast_to(most, (members, LANES - ends - CAP)),
        ],
        1,
    )
    second = exchange(second, "dev")
    got_listed = second[:, ends : ends + CAP]
    most = jnp.max(second[:, ends + CAP :])
    got_code = second[:, :ends].reshape(members, groups, CAP_E)
    got_code = jnp.transpose(got_code, (1, 0, 2)).reshape(groups, members * CAP_E)
    got_end = jnp.where(got_code >= 0, got_code & (SHIFT - 1), -1)
    got_count = jnp.where(got_code >= 0, got_code >> 16, 0)

    row_index = jnp.concatenate([got_near, got_end], 1).reshape(-1)
    rows = exchange(pick(row_index, mem_half).reshape(groups, -1, row_width), "grp")
    near_block = rows[:, :CAP_N].reshape(block, row_width)
    end_part = jnp.transpose(
        rows[:, CAP_N:].reshape(groups, members, CAP_E, row_width), (1, 0, 2, 3)
    ).reshape(members, ends, row_width)
    near_part = jnp.dot(
        hot(got_listed.reshape(-1), block, 1), near_block, preferred_element_type=jnp.float32
    ).reshape(members, CAP, row_width)
    listed_ends = jnp.einsum(
        "dcp,dpw->dcw",
        hot(got_listed - block, ends, 2),
        end_part,
        preferred_element_type=jnp.float32,
    )
    table = exchange((near_part + listed_ends).astype(jnp.bfloat16), "dev")
    table = table.reshape(members * CAP, row_width)

    def fetch(table, index):
        return (
            jnp.take(table, index[: 2 * K * events], axis=0, mode="clip"),
            jnp.take(table, index[2 * K * events :], axis=0, mode="clip"),
        )

    def whole():
        full = jnp.broadcast_to(near_block[None], (members, block, row_width))
        full = exchange(jnp.concatenate([full, end_part], 1), "dev")
        return fetch(
            full.reshape(members * places, row_width),
            jnp.where(member >= 0, member * places + place, 0),
        )

    near_rows, end_rows = lax.cond(most > CAP, whole, lambda: fetch(table, index))
    near_rows = near_rows.reshape(2, K, events, row_width)
    end_rows = end_rows.reshape(2, events, row_width)
    elapsed = (
        (event_time[None, :] - jnp.transpose(near_time)).astype(jnp.float32).reshape(2, K, events)
    )
    embedded, message = event_block(
        end_rows,
        near_rows,
        elapsed,
        counted,
        frequency,
        phases,
        query_weight,
        key_weight,
        value_weight,
        out_weight,
        out_bias,
        message_in,
        message_out,
    )
    message = message.reshape(-1, row_width)
    message_high = lax.reduce_precision(message, 8, 7)
    slot_sum = jnp.dot(
        end_hot, message_high.astype(jnp.bfloat16), preferred_element_type=jnp.float32
    ) + jnp.dot(
        end_hot, (message - message_high).astype(jnp.bfloat16), preferred_element_type=jnp.float32
    )
    news = exchange(
        slot_sum.astype(jnp.bfloat16).reshape(groups * members, CAP_E, row_width), ("grp", "dev")
    ).reshape(-1, row_width)
    owned = got_end.reshape(-1)
    owned_hot = hot(owned, nodes, 0)
    totals = jnp.dot(owned_hot, news, preferred_element_type=jnp.float32)
    counts = jnp.sum(
        jnp.where(
            owned[None, :] == jnp.arange(nodes)[:, None], got_count.reshape(1, -1), 0
        ),
        axis=1,
    ).astype(jnp.float32)
    new_memory = gru_update(
        memory, mem_half, totals, counts, input_weight, state_weight, update_bias
    )
    return (new_memory, jnp.concatenate([embedded[0], embedded[1]], 1))


def solution(mesh):
    in_specs = (
        P(("grp", "dev"), None),
        P(("grp", "dev"), None, None),
        P(("grp", "dev"), None, None),
        P(("grp", "dev"), None),
        P(("grp", "dev"), None),
        P(("grp", "dev"), None),
        P(("grp", "dev")),
        P(("grp", "dev"), None),
        P(),
        P(),
        P(),
        P(),
        P(),
        P(),
        P(),
        P(),
        P(),
        P(),
        P(),
        P(),
    )
    out_specs = (P(("grp", "dev"), None), P(("grp", "dev"), None))
    return jax.shard_map(local, mesh=mesh, in_specs=in_specs, out_specs=out_specs, check_vma=False)
```

```python
import math

import jax
import jax.numpy as jnp
from jax import lax
from jax.experimental import pallas as pl
from jax.experimental.pallas import tpu as pltpu
from jax.sharding import PartitionSpec as P

HEADS = 2
K = 10
CAP_E = 2
CAP_N = 16
CAP = 88
LANES = 128
SHIFT = 65536


def hot(index, size, axis):
    index = jnp.expand_dims(index, axis)
    grid = lax.broadcasted_iota(jnp.int32, index.shape[:axis] + (size,) + index.shape[axis + 1 :], axis)
    return (index == grid).astype(jnp.bfloat16)


def pick(index, table):
    return jnp.dot(hot(index, table.shape[0], 1), table, preferred_element_type=jnp.float32).astype(
        jnp.bfloat16
    )


def split_slot(value, members, slots):
    width = slots.bit_length() - 1
    owner = value >> width
    return owner & (members - 1), ((owner >> (members.bit_length() - 1)) << width) | (value & (slots - 1))


def exchange(x, axis):
    return lax.all_to_all(x, axis, split_axis=0, concat_axis=0, tiled=True)


def event_block(
    end_rows,
    near_rows,
    elapsed,
    near_count,
    frequency,
    phases,
    query_weight,
    key_weight,
    value_weight,
    out_weight,
    out_bias,
    message_in,
    message_out,
):
    events = end_rows.shape[1]
    row_width = end_rows.shape[-1]
    head_size = row_width // HEADS
    fixed_code = jnp.broadcast_to(
        jnp.cos(phases).astype(jnp.bfloat16), (2, events, phases.shape[0])
    )
    near_code = jnp.cos(elapsed[..., None] * frequency + phases).astype(jnp.bfloat16)
    query_in = jnp.concatenate([end_rows, fixed_code], -1)
    queries = jnp.einsum("jec,cd->jed", query_in, query_weight, preferred_element_type=jnp.float32)
    near_in = jnp.concatenate([near_rows, near_code], -1)
    key_rows = jnp.einsum("jkec,cd->jked", near_in, key_weight, preferred_element_type=jnp.float32)
    values = jnp.einsum("jkec,cd->jked", near_in, value_weight, preferred_element_type=jnp.float32)
    usable = jnp.arange(K)[None, :, None] < near_count[:, None, :]
    pieces = []
    for head in range(HEADS):
        low = head * head_size
        high = low + head_size
        scores = jnp.sum(
            queries[:, None, :, low:high] * key_rows[..., low:high], axis=-1
        ) / math.sqrt(head_size)
        exponent = jnp.where(usable, jnp.exp(scores), jnp.zeros_like(scores))
        weight = exponent / jnp.sum(exponent, axis=1, keepdims=True)
        pieces.append(jnp.sum(weight[..., None] * values[..., low:high], axis=1))
    attended = jnp.concatenate(pieces, -1).astype(jnp.bfloat16)
    joined = jnp.concatenate([attended, end_rows], -1)
    embedded = jax.nn.relu(
        jnp.einsum("jec,cd->jed", joined, out_weight, preferred_element_type=jnp.float32) + out_bias
    ).astype(jnp.bfloat16)
    paired = jnp.concatenate([embedded, embedded[::-1]], -1)
    hidden = jax.nn.relu(
        jnp.einsum("jec,cd->jed", paired, message_in, preferred_element_type=jnp.float32)
    ).astype(jnp.bfloat16)
    message = jnp.einsum("jec,cd->jed", hidden, message_out, preferred_element_type=jnp.float32)
    return (embedded, message)


def across(left, right):
    return lax.dot_general(
        left, right, (((1,), (1,)), ((), ())), preferred_element_type=jnp.float32
    )


def event_kernel(
    table,
    lanes,
    count,
    slot,
    code,
    fixed,
    query_weight,
    pair_weight,
    out_weight,
    out_bias,
    message_in,
    message_out,
    embedded,
    slot_sum,
    turned,
    values,
    exponents,
):
    rows, width = table.shape
    pairs = lanes.shape[1]
    events = pairs // 2
    head_size = width // HEADS
    one = jnp.bfloat16(1)
    none = jnp.bfloat16(0)

    def dot(left, right):
        return jnp.dot(left, right, preferred_element_type=jnp.float32)

    def number(size):
        return lax.broadcasted_iota(jnp.int32, (size, pairs), 0).astype(jnp.float32).astype(jnp.bfloat16)

    def near(index, first, size):
        return jnp.clip(index - first, -1, size).astype(jnp.float32).astype(jnp.bfloat16)

    row = lax.broadcasted_iota(jnp.int32, (width, width), 0)
    column = lax.broadcasted_iota(jnp.int32, (width, width), 1)
    unit = jnp.where(row == column, 1.0, 0.0).astype(jnp.bfloat16)
    for low in range(0, rows, width):
        turned[:, low : low + width] = across(unit, table[low : low + width, :]).astype(jnp.bfloat16)
    numbers = number(width)

    def gather(index):
        total = jnp.zeros((width, pairs), jnp.float32)
        for low in range(0, rows, width):
            chosen = jnp.where(numbers == near(index, low, width), one, none)
            total = total + dot(turned[:, low : low + width], chosen)
        return total.astype(jnp.bfloat16)

    ends = gather(lanes[K : K + 1, :])
    queries = dot(query_weight[:, :width], ends) + dot(query_weight[:, width:], fixed[...])

    def neighbour(k, carry):
        near_rows = gather(lanes[pl.ds(k, 1), :])
        pair = dot(pair_weight[:, :width], near_rows) + dot(pair_weight[:, width:], code[k])
        values[k] = pair[width:]
        product = queries * pair[:width]
        for head in range(HEADS):
            scores = jnp.sum(
                product[head * head_size : (head + 1) * head_size], axis=0, keepdims=True
            ) / math.sqrt(head_size)
            exponents[k, head : head + 1, :] = jnp.where(k < count[...], jnp.exp(scores), 0.0)
        return carry

    lax.fori_loop(0, K, neighbour, 0)
    pieces = []
    for head in range(HEADS):
        low = head * head_size
        high = low + head_size
        total = exponents[0, head : head + 1, :]
        for k in range(1, K):
            total = total + exponents[k, head : head + 1, :]
        piece = jnp.zeros((head_size, pairs), jnp.float32)
        for k in range(K):
            piece = piece + exponents[k, head : head + 1, :] / total * values[k, low:high, :]
        pieces.append(piece)
    attended = jnp.concatenate(pieces, 0).astype(jnp.bfloat16)
    embeds = jnp.maximum(
        dot(out_weight[:, :width], attended) + dot(out_weight[:, width:], ends) + out_bias[...], 0.0
    ).astype(jnp.bfloat16)
    other = jnp.concatenate([embeds[:, events:], embeds[:, :events]], 1)
    hidden = jnp.maximum(
        dot(message_in[:, :width], embeds) + dot(message_in[:, width:], other), 0.0
    ).astype(jnp.bfloat16)
    message = dot(message_out[...], hidden)
    high = message.astype(jnp.bfloat16)
    low = (message - high.astype(jnp.float32)).astype(jnp.bfloat16)
    for first in range(0, slot_sum.shape[0], width):
        chosen = jnp.where(numbers == near(slot[...], first, width), one, none)
        slot_sum[first : first + width, :] = (across(chosen, high) + across(chosen, low)).astype(
            jnp.bfloat16
        )
    for side in range(2):
        half = embeds[:, side * events : (side + 1) * events]
        embedded[:, side * width : (side + 1) * width] = across(
            unit[:events, :events], half
        ).astype(jnp.bfloat16)


def gru_update(memory, mem_half, totals, counts, input_weight, state_weight, update_bias):
    row_width = memory.shape[1]
    averaged = (totals / jnp.maximum(counts, 1.0)[:, None]).astype(jnp.bfloat16)
    from_msg = jnp.dot(averaged, input_weight, preferred_element_type=jnp.float32)
    from_state = jnp.dot(mem_half, state_weight, preferred_element_type=jnp.float32)
    update_gate = jax.nn.sigmoid(
        from_msg[:, :row_width] + from_state[:, :row_width] + update_bias[:row_width]
    )
    reset_gate = jax.nn.sigmoid(
        from_msg[:, row_width : 2 * row_width]
        + from_state[:, row_width : 2 * row_width]
        + update_bias[row_width : 2 * row_width]
    )
    candidate = jnp.tanh(
        from_msg[:, 2 * row_width :]
        + update_bias[2 * row_width :]
        + reset_gate * from_state[:, 2 * row_width :]
    )
    updated = (1.0 - update_gate) * candidate + update_gate * memory
    return jnp.where((counts > 0)[:, None], updated, memory)


def local(
    memory,
    want_end,
    want_near,
    end_slot,
    near_slot,
    near_count,
    event_time,
    near_time,
    frequency,
    phases,
    query_weight,
    key_weight,
    value_weight,
    out_weight,
    out_bias,
    message_in,
    message_out,
    input_weight,
    state_weight,
    update_bias,
):
    groups = lax.axis_size("grp")
    members = lax.axis_size("dev")
    nodes, row_width = memory.shape
    events = end_slot.shape[0]
    block = groups * CAP_N
    ends = groups * CAP_E
    places = block + ends
    mem_half = memory.astype(jnp.bfloat16)
    counted = jnp.transpose(near_count)

    near_value = jnp.transpose(near_slot).reshape(-1)
    end_value = jnp.transpose(end_slot).reshape(-1)
    near_member, near_place = split_slot(near_value, members, CAP_N)
    end_member, end_place = split_slot(end_value, members, CAP_E)
    usable = (jnp.arange(K)[None, :, None] < counted[:, None, :]).reshape(-1)
    member = jnp.concatenate([jnp.where(usable, near_member, -1), end_member])
    place = jnp.concatenate([near_place, end_place + block])
    member_hot = hot(member, members, 0)
    place_hot = hot(place, places, 0)
    used = (
        lax.dot_general(
            member_hot, place_hot, (((1,), (1,)), ((), ())), preferred_element_type=jnp.float32
        )
        > 0
    )
    before = (jnp.arange(places)[:, None] < jnp.arange(places)[None, :]).astype(jnp.bfloat16)
    rank = jnp.dot(used.astype(jnp.bfloat16), before, preferred_element_type=jnp.float32)
    most = jnp.max(jnp.sum(used.astype(jnp.int32), axis=1))
    rank_or_none = jnp.where(used, rank.astype(jnp.int32), -1)
    listed = jnp.sum(
        jnp.where(
            rank_or_none[:, None, :] == jnp.arange(CAP)[None, :, None],
            jnp.arange(places)[None, None, :],
            0,
        ),
        axis=2,
    )
    ref_rank = jnp.sum(
        jnp.dot(rank.astype(jnp.bfloat16), place_hot, preferred_element_type=jnp.float32)
        * member_hot.astype(jnp.float32),
        axis=0,
    ).astype(jnp.int32)
    index = jnp.where(member >= 0, member * CAP + jnp.minimum(ref_rank, CAP - 1), 0)

    end_hot = hot(end_value, groups * members * CAP_E, 0)
    slot_count = jnp.sum(end_hot.astype(jnp.float32), axis=1).astype(jnp.int32)
    wanted = want_end.reshape(-1)
    asked = jnp.where(wanted >= 0, wanted + SHIFT * slot_count, -1).reshape(groups, members * CAP_E)

    mine = lax.axis_index("dev")
    ask_near = lax.dynamic_index_in_dim(
        want_near.reshape(groups, members, CAP_N), mine, 1, keepdims=False
    )
    first = jnp.concatenate(
        [
            asked,
            ask_near,
            jnp.broadcast_to(most, (groups, LANES - members * CAP_E - CAP_N)),
        ],
        1,
    )
    first = exchange(first, "grp")
    got_near = first[:, members * CAP_E : members * CAP_E + CAP_N]
    most = jnp.max(first[:, members * CAP_E + CAP_N :])
    passed = jnp.transpose(
        first[:, : members * CAP_E].reshape(groups, members, CAP_E), (1, 0, 2)
    ).reshape(members, ends)
    second = jnp.concatenate(
        [
            passed,
            listed,
            jnp.broadcast_to(most, (members, LANES - ends - CAP)),
        ],
        1,
    )
    second = exchange(second, "dev")
    got_listed = second[:, ends : ends + CAP]
    most = jnp.max(second[:, ends + CAP :])
    got_code = second[:, :ends].reshape(members, groups, CAP_E)
    got_code = jnp.transpose(got_code, (1, 0, 2)).reshape(groups, members * CAP_E)
    got_end = jnp.where(got_code >= 0, got_code & (SHIFT - 1), -1)
    got_count = jnp.where(got_code >= 0, got_code >> 16, 0)

    row_index = jnp.concatenate([got_near, got_end], 1).reshape(-1)
    rows = exchange(pick(row_index, mem_half).reshape(groups, -1, row_width), "grp")
    near_block = rows[:, :CAP_N].reshape(block, row_width)
    end_part = jnp.transpose(
        rows[:, CAP_N:].reshape(groups, members, CAP_E, row_width), (1, 0, 2, 3)
    ).reshape(members, ends, row_width)
    near_part = jnp.dot(
        hot(got_listed.reshape(-1), block, 1), near_block, preferred_element_type=jnp.float32
    ).reshape(members, CAP, row_width)
    listed_ends = jnp.einsum(
        "dcp,dpw->dcw",
        hot(got_listed - block, ends, 2),
        end_part,
        preferred_element_type=jnp.float32,
    )
    table = exchange((near_part + listed_ends).astype(jnp.bfloat16), "dev")
    table = table.reshape(members * CAP, row_width)

    elapsed = (event_time[None, :] - jnp.transpose(near_time)).astype(jnp.float32)
    elapsed = elapsed.reshape(2, K, events)

    def whole():
        full = jnp.broadcast_to(near_block[None], (members, block, row_width))
        full = exchange(jnp.concatenate([full, end_part], 1), "dev")
        fetched = jnp.take(
            full.reshape(members * places, row_width),
            jnp.where(member >= 0, member * places + place, 0),
            axis=0,
            mode="clip",
        )
        embedded, message = event_block(
            fetched[2 * K * events :].reshape(2, events, row_width),
            fetched[: 2 * K * events].reshape(2, K, events, row_width),
            elapsed,
            counted,
            frequency,
            phases,
            query_weight,
            key_weight,
            value_weight,
            out_weight,
            out_bias,
            message_in,
            message_out,
        )
        message = message.reshape(-1, row_width)
        high = lax.reduce_precision(message, 8, 7)
        slot_sum = jnp.dot(
            end_hot, high.astype(jnp.bfloat16), preferred_element_type=jnp.float32
        ) + jnp.dot(
            end_hot, (message - high).astype(jnp.bfloat16), preferred_element_type=jnp.float32
        )
        return jnp.concatenate([embedded[0], embedded[1]], 1), slot_sum.astype(jnp.bfloat16)

    pairs = 2 * events
    near_lanes = jnp.transpose(index[: 2 * K * events].reshape(2, K, events), (1, 0, 2))
    lanes = jnp.concatenate(
        [near_lanes.reshape(K, pairs), index[2 * K * events :].reshape(1, pairs)], 0
    )
    elapsed_lanes = jnp.transpose(elapsed, (1, 0, 2)).reshape(K, 1, pairs)
    code = jnp.cos(elapsed_lanes * frequency[None, :, None] + phases[None, :, None])
    fixed = jnp.broadcast_to(jnp.cos(phases)[:, None], (phases.shape[0], pairs))
    operands = (
        lanes,
        counted.reshape(1, pairs),
        end_value.reshape(1, pairs),
        code.astype(jnp.bfloat16),
        fixed.astype(jnp.bfloat16),
        jnp.transpose(query_weight),
        jnp.transpose(jnp.concatenate([key_weight, value_weight], 1)),
        jnp.transpose(out_weight),
        out_bias[:, None],
        jnp.transpose(message_in),
        jnp.transpose(message_out),
    )

    def listed_only():
        return pl.pallas_call(
            event_kernel,
            out_shape=(
                jax.ShapeDtypeStruct((events, 2 * row_width), jnp.bfloat16),
                jax.ShapeDtypeStruct((groups * members * CAP_E, row_width), jnp.bfloat16),
            ),
            scratch_shapes=[
                pltpu.VMEM((row_width, table.shape[0]), jnp.bfloat16),
                pltpu.VMEM((K, row_width, pairs), jnp.float32),
                pltpu.VMEM((K, 8, pairs), jnp.float32),
            ],
            name="event_kernel",
        )(table, *operands)

    embedded, slot_sum = lax.cond(most > CAP, whole, listed_only)
    news = exchange(
        slot_sum.reshape(groups * members, CAP_E, row_width), ("grp", "dev")
    ).reshape(-1, row_width)
    owned = got_end.reshape(-1)
    owned_hot = hot(owned, nodes, 0)
    totals = jnp.dot(owned_hot, news, preferred_element_type=jnp.float32)
    counts = jnp.sum(
        jnp.where(
            owned[None, :] == jnp.arange(nodes)[:, None], got_count.reshape(1, -1), 0
        ),
        axis=1,
    ).astype(jnp.float32)
    new_memory = gru_update(
        memory, mem_half, totals, counts, input_weight, state_weight, update_bias
    )
    return (new_memory, embedded)


def solution(mesh):
    in_specs = (
        P(("grp", "dev"), None),
        P(("grp", "dev"), None, None),
        P(("grp", "dev"), None, None),
        P(("grp", "dev"), None),
        P(("grp", "dev"), None),
        P(("grp", "dev"), None),
        P(("grp", "dev")),
        P(("grp", "dev"), None),
        P(),
        P(),
        P(),
        P(),
        P(),
        P(),
        P(),
        P(),
        P(),
        P(),
        P(),
        P(),
    )
    out_specs = (P(("grp", "dev"), None), P(("grp", "dev"), None))
    return jax.shard_map(local, mesh=mesh, in_specs=in_specs, out_specs=out_specs, check_vma=False)
```

```python
import math

import jax
import jax.numpy as jnp
from jax import lax
from jax.experimental import pallas as pl
from jax.experimental.pallas import tpu as pltpu
from jax.sharding import PartitionSpec as P

HEADS = 2
K = 10
CAP_E = 2
CAP_N = 16
CAP = 88
LANES = 128
SHIFT = 65536


def hot(index, size, axis):
    index = jnp.expand_dims(index, axis)
    grid = lax.broadcasted_iota(jnp.int32, index.shape[:axis] + (size,) + index.shape[axis + 1 :], axis)
    return (index == grid).astype(jnp.bfloat16)


def pick(index, table):
    return jnp.dot(hot(index, table.shape[0], 1), table, preferred_element_type=jnp.float32).astype(
        jnp.bfloat16
    )


def split_slot(value, members, slots):
    width = slots.bit_length() - 1
    owner = value >> width
    return owner & (members - 1), ((owner >> (members.bit_length() - 1)) << width) | (value & (slots - 1))


def exchange(x, axis):
    return lax.all_to_all(x, axis, split_axis=0, concat_axis=0, tiled=True)


def event_block(
    end_rows,
    near_rows,
    elapsed,
    near_count,
    frequency,
    phases,
    query_weight,
    key_weight,
    value_weight,
    out_weight,
    out_bias,
    message_in,
    message_out,
):
    events = end_rows.shape[1]
    row_width = end_rows.shape[-1]
    head_size = row_width // HEADS
    fixed_code = jnp.broadcast_to(
        jnp.cos(phases).astype(jnp.bfloat16), (2, events, phases.shape[0])
    )
    near_code = jnp.cos(elapsed[..., None] * frequency + phases).astype(jnp.bfloat16)
    query_in = jnp.concatenate([end_rows, fixed_code], -1)
    queries = jnp.einsum("jec,cd->jed", query_in, query_weight, preferred_element_type=jnp.float32)
    near_in = jnp.concatenate([near_rows, near_code], -1)
    key_rows = jnp.einsum("jkec,cd->jked", near_in, key_weight, preferred_element_type=jnp.float32)
    values = jnp.einsum("jkec,cd->jked", near_in, value_weight, preferred_element_type=jnp.float32)
    usable = jnp.arange(K)[None, :, None] < near_count[:, None, :]
    pieces = []
    for head in range(HEADS):
        low = head * head_size
        high = low + head_size
        scores = jnp.sum(
            queries[:, None, :, low:high] * key_rows[..., low:high], axis=-1
        ) / math.sqrt(head_size)
        exponent = jnp.where(usable, jnp.exp(scores), jnp.zeros_like(scores))
        weight = exponent / jnp.sum(exponent, axis=1, keepdims=True)
        pieces.append(jnp.sum(weight[..., None] * values[..., low:high], axis=1))
    attended = jnp.concatenate(pieces, -1).astype(jnp.bfloat16)
    joined = jnp.concatenate([attended, end_rows], -1)
    embedded = jax.nn.relu(
        jnp.einsum("jec,cd->jed", joined, out_weight, preferred_element_type=jnp.float32) + out_bias
    ).astype(jnp.bfloat16)
    paired = jnp.concatenate([embedded, embedded[::-1]], -1)
    hidden = jax.nn.relu(
        jnp.einsum("jec,cd->jed", paired, message_in, preferred_element_type=jnp.float32)
    ).astype(jnp.bfloat16)
    message = jnp.einsum("jec,cd->jed", hidden, message_out, preferred_element_type=jnp.float32)
    return (embedded, message)


def across(left, right):
    return lax.dot_general(
        left, right, (((1,), (1,)), ((), ())), preferred_element_type=jnp.float32
    )


def request_kernel(mine, near_slot, end_slot, count, want_end, want_near, first, rank_or_none):
    groups = first.shape[0]
    members, places = rank_or_none.shape
    events = near_slot.shape[1]
    owners = groups * members
    block = groups * CAP_N

    def ones(match):
        return jnp.where(match, 1.0, 0.0).astype(jnp.bfloat16)

    def numbers(size, width):
        return lax.broadcasted_iota(jnp.int32, (size, width), 0)

    def lanes(size, width):
        return lax.broadcasted_iota(jnp.int32, (size, width), 1)

    member_pieces = []
    place_pieces = []
    for line in range(2 * K):
        member, place = split_slot(near_slot[line : line + 1, :], members, CAP_N)
        side = line // K
        member = jnp.where(line - side * K < count[side : side + 1, :], member, -1)
        member_pieces.append(ones(numbers(members, events) == member))
        place_pieces.append(ones(numbers(places, events) == place))
    group_pieces = []
    lane_pieces = []
    for line in range(2):
        value = end_slot[line : line + 1, :]
        member, place = split_slot(value, members, CAP_E)
        member_pieces.append(ones(numbers(members, events) == member))
        place_pieces.append(ones(numbers(places, events) == place + block))
        group = value >> (CAP_E * members).bit_length() - 1
        group_pieces.append(ones(numbers(groups, events) == group))
        lane_pieces.append(ones(numbers(LANES, events) == (value & (CAP_E - 1)) * members + member))
    uses = across(jnp.concatenate(member_pieces, 1), jnp.concatenate(place_pieces, 1))
    used = ones(uses > 0)
    before = ones(numbers(places, places) < lanes(places, places))
    rank = jnp.dot(used, before, preferred_element_type=jnp.float32)
    rank_or_none[...] = jnp.where(uses > 0, rank, -1.0).astype(jnp.int32)
    most = jnp.max(jnp.sum(used.astype(jnp.float32), axis=1, keepdims=True)).astype(jnp.int32)
    times = across(jnp.concatenate(group_pieces, 1), jnp.concatenate(lane_pieces, 1)).astype(jnp.int32)

    group = lanes(groups, owners) >> members.bit_length() - 1
    own = group == numbers(groups, owners)
    column = numbers(LANES, owners)
    owner = lanes(LANES, owners)

    def spread(part):
        total = jnp.zeros((groups, LANES), jnp.float32)
        for slot in range(CAP_E):
            row = part(want_end[slot : slot + 1, :])
            total = total + across(
                jnp.where(own, row, 0.0).astype(jnp.bfloat16),
                ones(column == slot * members + (owner & (members - 1))),
            )
        asked = jnp.concatenate(
            [
                jnp.zeros((members * CAP_E, owners), jnp.float32),
                part(want_near[...]),
                jnp.zeros((LANES - members * CAP_E - CAP_N, owners), jnp.float32),
            ],
            0,
        )
        return total + across(
            ones(own & ((lanes(groups, owners) & (members - 1)) == mine[0])),
            asked.astype(jnp.bfloat16),
        )

    high = spread(lambda wanted: ((wanted + 1) >> 4).astype(jnp.float32))
    low = spread(lambda wanted: ((wanted + 1) & 15).astype(jnp.float32))
    wanted = (16 * high + low).astype(jnp.int32) - 1
    lane = lanes(groups, LANES)
    wanted = jnp.where((lane < members * CAP_E) & (wanted >= 0), wanted + SHIFT * times, wanted)
    first[...] = jnp.where(lane < members * CAP_E + CAP_N, wanted, most)


def event_kernel(
    table,
    lanes,
    count,
    slot,
    code,
    fixed,
    query_weight,
    pair_weight,
    out_weight,
    out_bias,
    message_in,
    message_out,
    embedded,
    slot_sum,
    turned,
    values,
    exponents,
):
    rows, width = table.shape
    pairs = lanes.shape[1]
    events = pairs // 2
    head_size = width // HEADS
    one = jnp.bfloat16(1)
    none = jnp.bfloat16(0)

    def dot(left, right):
        return jnp.dot(left, right, preferred_element_type=jnp.float32)

    def number(size):
        return lax.broadcasted_iota(jnp.int32, (size, pairs), 0).astype(jnp.float32).astype(jnp.bfloat16)

    def near(index, first, size):
        return jnp.clip(index - first, -1, size).astype(jnp.float32).astype(jnp.bfloat16)

    row = lax.broadcasted_iota(jnp.int32, (width, width), 0)
    column = lax.broadcasted_iota(jnp.int32, (width, width), 1)
    unit = jnp.where(row == column, 1.0, 0.0).astype(jnp.bfloat16)
    for low in range(0, rows, width):
        turned[:, low : low + width] = across(unit, table[low : low + width, :]).astype(jnp.bfloat16)
    numbers = number(width)

    def gather(index):
        total = jnp.zeros((width, pairs), jnp.float32)
        for low in range(0, rows, width):
            chosen = jnp.where(numbers == near(index, low, width), one, none)
            total = total + dot(turned[:, low : low + width], chosen)
        return total.astype(jnp.bfloat16)

    ends = gather(lanes[K : K + 1, :])
    queries = dot(query_weight[:, :width], ends) + across(
        query_weight[:, width:], jnp.broadcast_to(fixed[...], (pairs, fixed.shape[1]))
    )

    def neighbour(k, carry):
        near_rows = gather(lanes[pl.ds(k, 1), :])
        pair = dot(pair_weight[:, :width], near_rows) + dot(pair_weight[:, width:], code[k])
        values[k] = pair[width:]
        product = queries * pair[:width]
        for head in range(HEADS):
            scores = jnp.sum(
                product[head * head_size : (head + 1) * head_size], axis=0, keepdims=True
            ) / math.sqrt(head_size)
            exponents[k, head : head + 1, :] = jnp.where(k < count[...], jnp.exp(scores), 0.0)
        return carry

    lax.fori_loop(0, K, neighbour, 0)
    pieces = []
    for head in range(HEADS):
        low = head * head_size
        high = low + head_size
        total = exponents[0, head : head + 1, :]
        for k in range(1, K):
            total = total + exponents[k, head : head + 1, :]
        piece = jnp.zeros((head_size, pairs), jnp.float32)
        for k in range(K):
            piece = piece + exponents[k, head : head + 1, :] / total * values[k, low:high, :]
        pieces.append(piece)
    attended = jnp.concatenate(pieces, 0).astype(jnp.bfloat16)
    embeds = jnp.maximum(
        dot(out_weight[:, :width], attended)
        + dot(out_weight[:, width:], ends)
        + jnp.transpose(jnp.broadcast_to(out_bias[...], (pairs, width))),
        0.0,
    ).astype(jnp.bfloat16)
    other = jnp.concatenate([embeds[:, events:], embeds[:, :events]], 1)
    hidden = jnp.maximum(
        dot(message_in[:, :width], embeds) + dot(message_in[:, width:], other), 0.0
    ).astype(jnp.bfloat16)
    message = dot(message_out[...], hidden)
    high = message.astype(jnp.bfloat16)
    low = (message - high.astype(jnp.float32)).astype(jnp.bfloat16)
    for first in range(0, slot_sum.shape[0], width):
        chosen = jnp.where(numbers == near(slot[...], first, width), one, none)
        slot_sum[first : first + width, :] = (across(chosen, high) + across(chosen, low)).astype(
            jnp.bfloat16
        )
    for side in range(2):
        half = embeds[:, side * events : (side + 1) * events]
        embedded[:, side * width : (side + 1) * width] = across(
            unit[:events, :events], half
        ).astype(jnp.bfloat16)


def gru_update(memory, mem_half, totals, counts, input_weight, state_weight, update_bias):
    row_width = memory.shape[1]
    averaged = (totals / jnp.maximum(counts, 1.0)[:, None]).astype(jnp.bfloat16)
    from_msg = jnp.dot(averaged, input_weight, preferred_element_type=jnp.float32)
    from_state = jnp.dot(mem_half, state_weight, preferred_element_type=jnp.float32)
    update_gate = jax.nn.sigmoid(
        from_msg[:, :row_width] + from_state[:, :row_width] + update_bias[:row_width]
    )
    reset_gate = jax.nn.sigmoid(
        from_msg[:, row_width : 2 * row_width]
        + from_state[:, row_width : 2 * row_width]
        + update_bias[row_width : 2 * row_width]
    )
    candidate = jnp.tanh(
        from_msg[:, 2 * row_width :]
        + update_bias[2 * row_width :]
        + reset_gate * from_state[:, 2 * row_width :]
    )
    updated = (1.0 - update_gate) * candidate + update_gate * memory
    return jnp.where((counts > 0)[:, None], updated, memory)


def local(
    memory,
    want_end,
    want_near,
    end_slot,
    near_slot,
    near_count,
    event_time,
    near_time,
    frequency,
    phases,
    query_weight,
    key_weight,
    value_weight,
    out_weight,
    out_bias,
    message_in,
    message_out,
    input_weight,
    state_weight,
    update_bias,
):
    groups = lax.axis_size("grp")
    members = lax.axis_size("dev")
    nodes, row_width = memory.shape
    events = end_slot.shape[0]
    block = groups * CAP_N
    ends = groups * CAP_E
    places = block + ends
    mem_half = memory.astype(jnp.bfloat16)
    counted = jnp.transpose(near_count)

    near_value = jnp.transpose(near_slot)
    end_value = jnp.transpose(end_slot)
    first, rank_or_none = pl.pallas_call(
        request_kernel,
        out_shape=(
            jax.ShapeDtypeStruct((groups, LANES), jnp.int32),
            jax.ShapeDtypeStruct((members, places), jnp.int32),
        ),
        in_specs=[pl.BlockSpec(memory_space=pltpu.SMEM)]
        + [pl.BlockSpec(memory_space=pltpu.VMEM)] * 5,
        name="request_kernel",
    )(
        lax.axis_index("dev").reshape(1),
        near_value,
        end_value,
        counted,
        jnp.transpose(want_end.reshape(-1, CAP_E)),
        jnp.transpose(want_near.reshape(-1, CAP_N)),
    )
    first = exchange(first, "grp")

    near_value = near_value.reshape(-1)
    end_value = end_value.reshape(-1)
    near_member, near_place = split_slot(near_value, members, CAP_N)
    end_member, end_place = split_slot(end_value, members, CAP_E)
    usable = (jnp.arange(K)[None, :, None] < counted[:, None, :]).reshape(-1)
    member = jnp.concatenate([jnp.where(usable, near_member, -1), end_member])
    place = jnp.concatenate([near_place, end_place + block])
    listed = jnp.sum(
        jnp.where(
            rank_or_none[:, None, :] == jnp.arange(CAP)[None, :, None],
            jnp.arange(places)[None, None, :],
            0,
        ),
        axis=2,
    )
    ref_rank = jnp.sum(
        jnp.dot(
            jnp.minimum(rank_or_none, CAP).astype(jnp.bfloat16),
            hot(place, places, 0),
            preferred_element_type=jnp.float32,
        )
        * hot(member, members, 0).astype(jnp.float32),
        axis=0,
    ).astype(jnp.int32)
    index = jnp.where(member >= 0, member * CAP + jnp.minimum(ref_rank, CAP - 1), 0)

    got_near = first[:, members * CAP_E : members * CAP_E + CAP_N]
    most = jnp.max(first[:, members * CAP_E + CAP_N :])
    passed = jnp.transpose(
        first[:, : members * CAP_E].reshape(groups, CAP_E, members), (2, 0, 1)
    ).reshape(members, ends)
    second = jnp.concatenate(
        [
            passed,
            listed,
            jnp.broadcast_to(most, (members, LANES - ends - CAP)),
        ],
        1,
    )
    second = exchange(second, "dev")
    got_listed = second[:, ends : ends + CAP]
    most = jnp.max(second[:, ends + CAP :])
    got_code = second[:, :ends].reshape(members, groups, CAP_E)
    got_code = jnp.transpose(got_code, (1, 0, 2)).reshape(groups, members * CAP_E)
    got_end = jnp.where(got_code >= 0, got_code & (SHIFT - 1), -1)
    got_count = jnp.where(got_code >= 0, got_code >> 16, 0)

    row_index = jnp.concatenate([got_near, got_end], 1).reshape(-1)
    rows = exchange(pick(row_index, mem_half).reshape(groups, -1, row_width), "grp")
    near_block = rows[:, :CAP_N].reshape(block, row_width)
    end_part = jnp.transpose(
        rows[:, CAP_N:].reshape(groups, members, CAP_E, row_width), (1, 0, 2, 3)
    ).reshape(members, ends, row_width)
    near_part = jnp.dot(
        hot(got_listed.reshape(-1), block, 1), near_block, preferred_element_type=jnp.float32
    ).reshape(members, CAP, row_width)
    listed_ends = jnp.einsum(
        "dcp,dpw->dcw",
        hot(got_listed - block, ends, 2),
        end_part,
        preferred_element_type=jnp.float32,
    )
    table = exchange((near_part + listed_ends).astype(jnp.bfloat16), "dev")
    table = table.reshape(members * CAP, row_width)

    elapsed = (event_time[None, :] - jnp.transpose(near_time)).astype(jnp.float32)
    elapsed = elapsed.reshape(2, K, events)

    def whole():
        full = jnp.broadcast_to(near_block[None], (members, block, row_width))
        full = exchange(jnp.concatenate([full, end_part], 1), "dev")
        fetched = jnp.take(
            full.reshape(members * places, row_width),
            jnp.where(member >= 0, member * places + place, 0),
            axis=0,
            mode="clip",
        )
        embedded, message = event_block(
            fetched[2 * K * events :].reshape(2, events, row_width),
            fetched[: 2 * K * events].reshape(2, K, events, row_width),
            elapsed,
            counted,
            frequency,
            phases,
            query_weight,
            key_weight,
            value_weight,
            out_weight,
            out_bias,
            message_in,
            message_out,
        )
        message = message.reshape(-1, row_width)
        high = lax.reduce_precision(message, 8, 7)
        end_hot = hot(end_value, groups * members * CAP_E, 0)
        slot_sum = jnp.dot(
            end_hot, high.astype(jnp.bfloat16), preferred_element_type=jnp.float32
        ) + jnp.dot(
            end_hot, (message - high).astype(jnp.bfloat16), preferred_element_type=jnp.float32
        )
        return jnp.concatenate([embedded[0], embedded[1]], 1), slot_sum.astype(jnp.bfloat16)

    pairs = 2 * events
    near_lanes = jnp.transpose(index[: 2 * K * events].reshape(2, K, events), (1, 0, 2))
    lanes = jnp.concatenate(
        [near_lanes.reshape(K, pairs), index[2 * K * events :].reshape(1, pairs)], 0
    )
    elapsed_lanes = jnp.transpose(elapsed, (1, 0, 2)).reshape(K, 1, pairs)
    code = jnp.cos(elapsed_lanes * frequency[None, :, None] + phases[None, :, None])
    fixed = jnp.cos(phases)[None, :]
    operands = (
        lanes,
        counted.reshape(1, pairs),
        end_value.reshape(1, pairs),
        code.astype(jnp.bfloat16),
        fixed.astype(jnp.bfloat16),
        jnp.transpose(query_weight),
        jnp.transpose(jnp.concatenate([key_weight, value_weight], 1)),
        jnp.transpose(out_weight),
        out_bias[None, :],
        jnp.transpose(message_in),
        jnp.transpose(message_out),
    )

    def listed_only():
        return pl.pallas_call(
            event_kernel,
            out_shape=(
                jax.ShapeDtypeStruct((events, 2 * row_width), jnp.bfloat16),
                jax.ShapeDtypeStruct((groups * members * CAP_E, row_width), jnp.bfloat16),
            ),
            scratch_shapes=[
                pltpu.VMEM((row_width, table.shape[0]), jnp.bfloat16),
                pltpu.VMEM((K, row_width, pairs), jnp.float32),
                pltpu.VMEM((K, 8, pairs), jnp.float32),
            ],
            name="event_kernel",
        )(table, *operands)

    embedded, slot_sum = lax.cond(most > CAP, whole, listed_only)
    news = exchange(
        slot_sum.reshape(groups * members, CAP_E, row_width), ("grp", "dev")
    ).reshape(-1, row_width)
    owned = got_end.reshape(-1)
    owned_hot = hot(owned, nodes, 0)
    totals = jnp.dot(owned_hot, news, preferred_element_type=jnp.float32)
    counts = jnp.sum(
        jnp.where(
            owned[None, :] == jnp.arange(nodes)[:, None], got_count.reshape(1, -1), 0
        ),
        axis=1,
    ).astype(jnp.float32)
    new_memory = gru_update(
        memory, mem_half, totals, counts, input_weight, state_weight, update_bias
    )
    return (new_memory, embedded)


def solution(mesh):
    in_specs = (
        P(("grp", "dev"), None),
        P(("grp", "dev"), None, None),
        P(("grp", "dev"), None, None),
        P(("grp", "dev"), None),
        P(("grp", "dev"), None),
        P(("grp", "dev"), None),
        P(("grp", "dev")),
        P(("grp", "dev"), None),
        P(),
        P(),
        P(),
        P(),
        P(),
        P(),
        P(),
        P(),
        P(),
        P(),
        P(),
        P(),
    )
    out_specs = (P(("grp", "dev"), None), P(("grp", "dev"), None))
    return jax.shard_map(local, mesh=mesh, in_specs=in_specs, out_specs=out_specs, check_vma=False)
```

```python
import math

import jax
import jax.numpy as jnp
from jax import lax
from jax.experimental import pallas as pl
from jax.experimental.pallas import tpu as pltpu
from jax.sharding import PartitionSpec as P

HEADS = 2
K = 10
CAP_E = 2
CAP_N = 16
CAP = 87
CAP_SUM = 24
CAP_OWN = 31
LANES = 128
SHIFT = 65536


def hot(index, size, axis):
    index = jnp.expand_dims(index, axis)
    grid = lax.broadcasted_iota(jnp.int32, index.shape[:axis] + (size,) + index.shape[axis + 1 :], axis)
    return (index == grid).astype(jnp.bfloat16)


def pick(index, table):
    return jnp.dot(hot(index, table.shape[0], 1), table, preferred_element_type=jnp.float32).astype(
        jnp.bfloat16
    )


def split_slot(value, members, slots):
    width = slots.bit_length() - 1
    owner = value >> width
    return owner & (members - 1), ((owner >> (members.bit_length() - 1)) << width) | (value & (slots - 1))


def ranks(marks):
    size = marks.shape[1]
    before = (jnp.arange(size)[:, None] < jnp.arange(size)[None, :]).astype(jnp.bfloat16)
    rank = jnp.dot(marks.astype(jnp.bfloat16), before, preferred_element_type=jnp.float32)
    full = jnp.sum(marks.astype(jnp.int32), axis=1) > CAP_OWN
    return jnp.where(marks, rank.astype(jnp.int32), -1), full.astype(jnp.float32)


def listing(rank, value, size):
    found = rank[:, None, :] == jnp.arange(size)[None, :, None]
    return jnp.sum(jnp.where(found, value[:, None, :] + 1, 0), axis=2) - 1


def flagged(rows, flag):
    last = jnp.arange(rows.shape[1])[None, :, None] == rows.shape[1] - 1
    return jnp.where(last, flag.astype(rows.dtype), rows)


def exchange(x, axis):
    return lax.all_to_all(x, axis, split_axis=0, concat_axis=0, tiled=True)


def event_block(
    end_rows,
    near_rows,
    elapsed,
    near_count,
    frequency,
    phases,
    query_weight,
    key_weight,
    value_weight,
    out_weight,
    out_bias,
    message_in,
    message_out,
):
    events = end_rows.shape[1]
    row_width = end_rows.shape[-1]
    head_size = row_width // HEADS
    fixed_code = jnp.broadcast_to(
        jnp.cos(phases).astype(jnp.bfloat16), (2, events, phases.shape[0])
    )
    near_code = jnp.cos(elapsed[..., None] * frequency + phases).astype(jnp.bfloat16)
    query_in = jnp.concatenate([end_rows, fixed_code], -1)
    queries = jnp.einsum("jec,cd->jed", query_in, query_weight, preferred_element_type=jnp.float32)
    near_in = jnp.concatenate([near_rows, near_code], -1)
    key_rows = jnp.einsum("jkec,cd->jked", near_in, key_weight, preferred_element_type=jnp.float32)
    values = jnp.einsum("jkec,cd->jked", near_in, value_weight, preferred_element_type=jnp.float32)
    usable = jnp.arange(K)[None, :, None] < near_count[:, None, :]
    pieces = []
    for head in range(HEADS):
        low = head * head_size
        high = low + head_size
        scores = jnp.sum(
            queries[:, None, :, low:high] * key_rows[..., low:high], axis=-1
        ) / math.sqrt(head_size)
        exponent = jnp.where(usable, jnp.exp(scores), jnp.zeros_like(scores))
        weight = exponent / jnp.sum(exponent, axis=1, keepdims=True)
        pieces.append(jnp.sum(weight[..., None] * values[..., low:high], axis=1))
    attended = jnp.concatenate(pieces, -1).astype(jnp.bfloat16)
    joined = jnp.concatenate([attended, end_rows], -1)
    embedded = jax.nn.relu(
        jnp.einsum("jec,cd->jed", joined, out_weight, preferred_element_type=jnp.float32) + out_bias
    ).astype(jnp.bfloat16)
    paired = jnp.concatenate([embedded, embedded[::-1]], -1)
    hidden = jax.nn.relu(
        jnp.einsum("jec,cd->jed", paired, message_in, preferred_element_type=jnp.float32)
    ).astype(jnp.bfloat16)
    message = jnp.einsum("jec,cd->jed", hidden, message_out, preferred_element_type=jnp.float32)
    return (embedded, message)


def across(left, right):
    return lax.dot_general(
        left, right, (((1,), (1,)), ((), ())), preferred_element_type=jnp.float32
    )


def request_kernel(mine, near_slot, end_slot, count, want_end, want_near, first, rank_or_none):
    groups = first.shape[0]
    members, places = rank_or_none.shape
    events = near_slot.shape[1]
    owners = groups * members
    block = groups * CAP_N

    def ones(match):
        return jnp.where(match, 1.0, 0.0).astype(jnp.bfloat16)

    def numbers(size, width):
        return lax.broadcasted_iota(jnp.int32, (size, width), 0)

    def lanes(size, width):
        return lax.broadcasted_iota(jnp.int32, (size, width), 1)

    member_pieces = []
    place_pieces = []
    for line in range(2 * K):
        member, place = split_slot(near_slot[line : line + 1, :], members, CAP_N)
        side = line // K
        member = jnp.where(line - side * K < count[side : side + 1, :], member, -1)
        member_pieces.append(ones(numbers(members, events) == member))
        place_pieces.append(ones(numbers(places, events) == place))
    group_pieces = []
    lane_pieces = []
    for line in range(2):
        value = end_slot[line : line + 1, :]
        member, place = split_slot(value, members, CAP_E)
        member_pieces.append(ones(numbers(members, events) == member))
        place_pieces.append(ones(numbers(places, events) == place + block))
        group = value >> (CAP_E * members).bit_length() - 1
        group_pieces.append(ones(numbers(groups, events) == group))
        lane_pieces.append(ones(numbers(LANES, events) == (value & (CAP_E - 1)) * members + member))
    uses = across(jnp.concatenate(member_pieces, 1), jnp.concatenate(place_pieces, 1))
    used = ones(uses > 0)
    before = ones(numbers(places, places) < lanes(places, places))
    rank = jnp.dot(used, before, preferred_element_type=jnp.float32)
    rank_or_none[...] = jnp.where(uses > 0, rank, -1.0).astype(jnp.int32)
    most = jnp.max(jnp.sum(used.astype(jnp.float32), axis=1, keepdims=True))
    most_ends = jnp.max(
        jnp.sum(
            jnp.where(lanes(members, places) >= block, used.astype(jnp.float32), 0.0), axis=1, keepdims=True
        )
    )
    most = jnp.where(most_ends > CAP_SUM, float(places), most).astype(jnp.int32)
    times = across(jnp.concatenate(group_pieces, 1), jnp.concatenate(lane_pieces, 1)).astype(jnp.int32)

    group = lanes(groups, owners) >> members.bit_length() - 1
    own = group == numbers(groups, owners)
    column = numbers(LANES, owners)
    owner = lanes(LANES, owners)

    def spread(part):
        total = jnp.zeros((groups, LANES), jnp.float32)
        for slot in range(CAP_E):
            row = part(want_end[slot : slot + 1, :])
            total = total + across(
                jnp.where(own, row, 0.0).astype(jnp.bfloat16),
                ones(column == slot * members + (owner & (members - 1))),
            )
        asked = jnp.concatenate(
            [
                jnp.zeros((members * CAP_E, owners), jnp.float32),
                part(want_near[...]),
                jnp.zeros((LANES - members * CAP_E - CAP_N, owners), jnp.float32),
            ],
            0,
        )
        return total + across(
            ones(own & ((lanes(groups, owners) & (members - 1)) == mine[0])),
            asked.astype(jnp.bfloat16),
        )

    high = spread(lambda wanted: ((wanted + 1) >> 4).astype(jnp.float32))
    low = spread(lambda wanted: ((wanted + 1) & 15).astype(jnp.float32))
    wanted = (16 * high + low).astype(jnp.int32) - 1
    lane = lanes(groups, LANES)
    wanted = jnp.where((lane < members * CAP_E) & (wanted >= 0), wanted + SHIFT * times, wanted)
    first[...] = jnp.where(lane < members * CAP_E + CAP_N, wanted, most)


def event_kernel(
    table,
    lanes,
    count,
    slot,
    code,
    fixed,
    query_weight,
    pair_weight,
    out_weight,
    out_bias,
    message_in,
    message_out,
    embedded,
    slot_sum,
    turned,
    values,
    exponents,
):
    rows, width = table.shape
    pairs = lanes.shape[1]
    events = pairs // 2
    head_size = width // HEADS
    one = jnp.bfloat16(1)
    none = jnp.bfloat16(0)

    def dot(left, right):
        return jnp.dot(left, right, preferred_element_type=jnp.float32)

    def number(size):
        return lax.broadcasted_iota(jnp.int32, (size, pairs), 0).astype(jnp.float32).astype(jnp.bfloat16)

    def near(index, first, size):
        return jnp.clip(index - first, -1, size).astype(jnp.float32).astype(jnp.bfloat16)

    row = lax.broadcasted_iota(jnp.int32, (width, width), 0)
    column = lax.broadcasted_iota(jnp.int32, (width, width), 1)
    unit = jnp.where(row == column, 1.0, 0.0).astype(jnp.bfloat16)
    for low in range(0, rows, width):
        turned[:, low : low + width] = across(unit, table[low : low + width, :]).astype(jnp.bfloat16)
    numbers = number(width)

    def gather(index):
        total = jnp.zeros((width, pairs), jnp.float32)
        for low in range(0, rows, width):
            chosen = jnp.where(numbers == near(index, low, width), one, none)
            total = total + dot(turned[:, low : low + width], chosen)
        return total.astype(jnp.bfloat16)

    ends = gather(lanes[K : K + 1, :])
    queries = dot(query_weight[:, :width], ends) + across(
        query_weight[:, width:], jnp.broadcast_to(fixed[...], (pairs, fixed.shape[1]))
    )

    def neighbour(k, carry):
        near_rows = gather(lanes[pl.ds(k, 1), :])
        pair = dot(pair_weight[:, :width], near_rows) + dot(pair_weight[:, width:], code[k])
        values[k] = pair[width:]
        product = queries * pair[:width]
        for head in range(HEADS):
            scores = jnp.sum(
                product[head * head_size : (head + 1) * head_size], axis=0, keepdims=True
            ) / math.sqrt(head_size)
            exponents[k, head : head + 1, :] = jnp.where(k < count[...], jnp.exp(scores), 0.0)
        return carry

    lax.fori_loop(0, K, neighbour, 0)
    pieces = []
    for head in range(HEADS):
        low = head * head_size
        high = low + head_size
        total = exponents[0, head : head + 1, :]
        for k in range(1, K):
            total = total + exponents[k, head : head + 1, :]
        piece = jnp.zeros((head_size, pairs), jnp.float32)
        for k in range(K):
            piece = piece + exponents[k, head : head + 1, :] / total * values[k, low:high, :]
        pieces.append(piece)
    attended = jnp.concatenate(pieces, 0).astype(jnp.bfloat16)
    embeds = jnp.maximum(
        dot(out_weight[:, :width], attended)
        + dot(out_weight[:, width:], ends)
        + jnp.transpose(jnp.broadcast_to(out_bias[...], (pairs, width))),
        0.0,
    ).astype(jnp.bfloat16)
    other = jnp.concatenate([embeds[:, events:], embeds[:, :events]], 1)
    hidden = jnp.maximum(
        dot(message_in[:, :width], embeds) + dot(message_in[:, width:], other), 0.0
    ).astype(jnp.bfloat16)
    message = dot(message_out[...], hidden)
    high = message.astype(jnp.bfloat16)
    low = (message - high.astype(jnp.float32)).astype(jnp.bfloat16)
    for first in range(0, slot_sum.shape[0], width):
        chosen = jnp.where(numbers == near(slot[...], first, width), one, none)
        slot_sum[first : first + width, :] = (across(chosen, high) + across(chosen, low)).astype(
            jnp.bfloat16
        )
    for side in range(2):
        half = embeds[:, side * events : (side + 1) * events]
        embedded[:, side * width : (side + 1) * width] = across(
            unit[:events, :events], half
        ).astype(jnp.bfloat16)


def gru_update(memory, mem_half, totals, counts, input_weight, state_weight, update_bias):
    row_width = memory.shape[1]
    averaged = (totals / jnp.maximum(counts, 1.0)[:, None]).astype(jnp.bfloat16)
    from_msg = jnp.dot(averaged, input_weight, preferred_element_type=jnp.float32)
    from_state = jnp.dot(mem_half, state_weight, preferred_element_type=jnp.float32)
    update_gate = jax.nn.sigmoid(
        from_msg[:, :row_width] + from_state[:, :row_width] + update_bias[:row_width]
    )
    reset_gate = jax.nn.sigmoid(
        from_msg[:, row_width : 2 * row_width]
        + from_state[:, row_width : 2 * row_width]
        + update_bias[row_width : 2 * row_width]
    )
    candidate = jnp.tanh(
        from_msg[:, 2 * row_width :]
        + update_bias[2 * row_width :]
        + reset_gate * from_state[:, 2 * row_width :]
    )
    updated = (1.0 - update_gate) * candidate + update_gate * memory
    return jnp.where((counts > 0)[:, None], updated, memory)


def local(
    memory,
    want_end,
    want_near,
    end_slot,
    near_slot,
    near_count,
    event_time,
    near_time,
    frequency,
    phases,
    query_weight,
    key_weight,
    value_weight,
    out_weight,
    out_bias,
    message_in,
    message_out,
    input_weight,
    state_weight,
    update_bias,
):
    groups = lax.axis_size("grp")
    members = lax.axis_size("dev")
    nodes, row_width = memory.shape
    events = end_slot.shape[0]
    block = groups * CAP_N
    ends = groups * CAP_E
    places = block + ends
    mem_half = memory.astype(jnp.bfloat16)
    counted = jnp.transpose(near_count)

    near_value = jnp.transpose(near_slot)
    end_value = jnp.transpose(end_slot)
    first, rank_or_none = pl.pallas_call(
        request_kernel,
        out_shape=(
            jax.ShapeDtypeStruct((groups, LANES), jnp.int32),
            jax.ShapeDtypeStruct((members, places), jnp.int32),
        ),
        in_specs=[pl.BlockSpec(memory_space=pltpu.SMEM)]
        + [pl.BlockSpec(memory_space=pltpu.VMEM)] * 5,
        name="request_kernel",
    )(
        lax.axis_index("dev").reshape(1),
        near_value,
        end_value,
        counted,
        jnp.transpose(want_end.reshape(-1, CAP_E)),
        jnp.transpose(want_near.reshape(-1, CAP_N)),
    )
    first = exchange(first, "grp")

    near_value = near_value.reshape(-1)
    end_value = end_value.reshape(-1)
    near_member, near_place = split_slot(near_value, members, CAP_N)
    end_member, end_place = split_slot(end_value, members, CAP_E)
    usable = (jnp.arange(K)[None, :, None] < counted[:, None, :]).reshape(-1)
    member = jnp.concatenate([jnp.where(usable, near_member, -1), end_member])
    place = jnp.concatenate([near_place, end_place + block])
    listed = jnp.sum(
        jnp.where(
            rank_or_none[:, None, :] == jnp.arange(CAP)[None, :, None],
            jnp.arange(places)[None, None, :],
            0,
        ),
        axis=2,
    )
    ref_rank = jnp.sum(
        jnp.dot(
            jnp.minimum(rank_or_none, CAP).astype(jnp.bfloat16),
            hot(place, places, 0),
            preferred_element_type=jnp.float32,
        )
        * hot(member, members, 0).astype(jnp.float32),
        axis=0,
    ).astype(jnp.int32)
    index = jnp.where(member >= 0, member * (CAP + 1) + jnp.minimum(ref_rank, CAP), 0)
    near_used = jnp.sum((rank_or_none[:, :block] >= 0).astype(jnp.int32), axis=1)
    sum_slot = end_member * CAP_SUM + ref_rank[2 * K * events :]
    sum_slot = sum_slot - jnp.sum(
        jnp.where(end_member[None, :] == jnp.arange(members)[:, None], near_used[:, None], 0), axis=0
    )

    got_near = first[:, members * CAP_E : members * CAP_E + CAP_N]
    most = jnp.max(first[:, members * CAP_E + CAP_N :])
    passed = jnp.transpose(
        first[:, : members * CAP_E].reshape(groups, CAP_E, members), (2, 0, 1)
    ).reshape(members, ends)
    second = jnp.concatenate(
        [
            passed,
            listed,
            jnp.broadcast_to(most, (members, LANES - ends - CAP)),
        ],
        1,
    )
    second = exchange(second, "dev")
    got_listed = second[:, ends : ends + CAP]
    most = jnp.max(second[:, ends + CAP :])
    got_code = second[:, :ends].reshape(members, groups, CAP_E)
    got_code = jnp.transpose(got_code, (1, 0, 2)).reshape(groups, members * CAP_E)
    got_end = jnp.where(got_code >= 0, got_code & (SHIFT - 1), -1)
    got_count = jnp.where(got_code >= 0, got_code >> 16, 0)

    own_rank, own_flag = ranks(got_count > 0)
    own_list = listing(own_rank, got_end, CAP_OWN)
    flag = jnp.max(own_flag)
    marked = jnp.any(
        got_listed[:, None, :] == block + jnp.arange(ends)[None, :, None], axis=2
    )
    place_rank = jnp.dot(
        marked.astype(jnp.bfloat16),
        (jnp.arange(ends)[:, None] < jnp.arange(ends)[None, :]).astype(jnp.bfloat16),
        preferred_element_type=jnp.float32,
    ).astype(jnp.int32)

    def by_group(x):
        return jnp.transpose(x.reshape(members, groups, CAP_E), (1, 0, 2)).reshape(groups, -1)

    relay_rank, _ = ranks(by_group(marked))
    sum_row = jnp.arange(members)[:, None] * CAP_SUM + jnp.minimum(place_rank, CAP_SUM - 1)
    relay_list = listing(relay_rank, by_group(sum_row), CAP_OWN + 1)
    per_group = CAP_N + CAP_OWN + 1
    end_row = jnp.arange(groups)[:, None] * per_group + CAP_N + jnp.minimum(relay_rank, CAP_OWN - 1)
    end_row = jnp.transpose(end_row.reshape(groups, members, CAP_E), (1, 0, 2)).reshape(members, ends)
    listed_row = jnp.where(
        got_listed < block,
        (got_listed // CAP_N) * per_group + got_listed % CAP_N,
        jnp.sum(
            jnp.where(
                got_listed[:, :, None] == block + jnp.arange(ends)[None, None, :],
                end_row[:, None, :],
                0,
            ),
            axis=2,
        ),
    )
    listed_row = jnp.concatenate([listed_row, jnp.full((members, 1), -1, jnp.int32)], 1)

    row_index = jnp.concatenate([got_near, own_list, jnp.full((groups, 1), -1, jnp.int32)], 1)
    rows = pick(row_index.reshape(-1), mem_half).reshape(groups, per_group, row_width)
    rows = exchange(flagged(rows, flag), "grp")
    flag = jnp.max(rows[:, per_group - 1, 0].astype(jnp.float32))
    rows = rows.reshape(groups * per_group, row_width)
    table = pick(listed_row.reshape(-1), rows).reshape(members, CAP + 1, row_width)
    table = exchange(flagged(table, flag), "dev")
    flag = jnp.max(table[:, CAP, 0].astype(jnp.float32))
    table = table.reshape(members * (CAP + 1), row_width)

    elapsed = (event_time[None, :] - jnp.transpose(near_time)).astype(jnp.float32)
    elapsed = elapsed.reshape(2, K, events)

    def whole():
        all_rows = pick(
            jnp.concatenate([got_near, got_end], 1).reshape(-1), mem_half
        ).reshape(groups, -1, row_width)
        all_rows = exchange(all_rows, "grp")
        full = jnp.broadcast_to(
            all_rows[:, :CAP_N].reshape(1, block, row_width), (members, block, row_width)
        )
        end_part = jnp.transpose(
            all_rows[:, CAP_N:].reshape(groups, members, CAP_E, row_width), (1, 0, 2, 3)
        ).reshape(members, ends, row_width)
        full = exchange(jnp.concatenate([full, end_part], 1), "dev")
        fetched = jnp.take(
            full.reshape(members * places, row_width),
            jnp.where(member >= 0, member * places + place, 0),
            axis=0,
            mode="clip",
        )
        embedded, message = event_block(
            fetched[2 * K * events :].reshape(2, events, row_width),
            fetched[: 2 * K * events].reshape(2, K, events, row_width),
            elapsed,
            counted,
            frequency,
            phases,
            query_weight,
            key_weight,
            value_weight,
            out_weight,
            out_bias,
            message_in,
            message_out,
        )
        message = message.reshape(-1, row_width)
        high = lax.reduce_precision(message, 8, 7)
        end_hot = hot(end_value, groups * members * CAP_E, 0)
        slot_sum = jnp.dot(
            end_hot, high.astype(jnp.bfloat16), preferred_element_type=jnp.float32
        ) + jnp.dot(
            end_hot, (message - high).astype(jnp.bfloat16), preferred_element_type=jnp.float32
        )
        news = exchange(
            slot_sum.astype(jnp.bfloat16).reshape(groups * members, CAP_E, row_width), ("grp", "dev")
        ).reshape(-1, row_width)
        totals = jnp.dot(
            hot(got_end.reshape(-1), nodes, 0), news, preferred_element_type=jnp.float32
        )
        return jnp.concatenate([embedded[0], embedded[1]], 1), totals

    pairs = 2 * events
    near_lanes = jnp.transpose(index[: 2 * K * events].reshape(2, K, events), (1, 0, 2))
    lanes = jnp.concatenate(
        [near_lanes.reshape(K, pairs), index[2 * K * events :].reshape(1, pairs)], 0
    )
    elapsed_lanes = jnp.transpose(elapsed, (1, 0, 2)).reshape(K, 1, pairs)
    code = jnp.cos(elapsed_lanes * frequency[None, :, None] + phases[None, :, None])
    fixed = jnp.cos(phases)[None, :]
    operands = (
        lanes,
        counted.reshape(1, pairs),
        sum_slot.reshape(1, pairs),
        code.astype(jnp.bfloat16),
        fixed.astype(jnp.bfloat16),
        jnp.transpose(query_weight),
        jnp.transpose(jnp.concatenate([key_weight, value_weight], 1)),
        jnp.transpose(out_weight),
        out_bias[None, :],
        jnp.transpose(message_in),
        jnp.transpose(message_out),
    )

    def listed_only():
        embedded, sums = pl.pallas_call(
            event_kernel,
            out_shape=(
                jax.ShapeDtypeStruct((events, 2 * row_width), jnp.bfloat16),
                jax.ShapeDtypeStruct((members * CAP_SUM, row_width), jnp.bfloat16),
            ),
            scratch_shapes=[
                pltpu.VMEM((row_width, table.shape[0]), jnp.bfloat16),
                pltpu.VMEM((K, row_width, pairs), jnp.float32),
                pltpu.VMEM((K, 8, pairs), jnp.float32),
            ],
            name="event_kernel",
        )(table, *operands)
        sums = exchange(sums.reshape(members, CAP_SUM, row_width), "dev")
        sums = pick(relay_list.reshape(-1), sums.reshape(members * CAP_SUM, row_width))
        news = exchange(sums.reshape(groups, CAP_OWN + 1, row_width), "grp")
        owned = jnp.concatenate([own_list, jnp.full((groups, 1), -1, jnp.int32)], 1)
        totals = jnp.dot(
            hot(owned.reshape(-1), nodes, 0),
            news.reshape(-1, row_width),
            preferred_element_type=jnp.float32,
        )
        return embedded, totals

    embedded, totals = lax.cond((most > CAP) | (flag > 0), whole, listed_only)
    owned = got_end.reshape(-1)
    counts = jnp.sum(
        jnp.where(
            owned[None, :] == jnp.arange(nodes)[:, None], got_count.reshape(1, -1), 0
        ),
        axis=1,
    ).astype(jnp.float32)
    new_memory = gru_update(
        memory, mem_half, totals, counts, input_weight, state_weight, update_bias
    )
    return (new_memory, embedded)


def solution(mesh):
    in_specs = (
        P(("grp", "dev"), None),
        P(("grp", "dev"), None, None),
        P(("grp", "dev"), None, None),
        P(("grp", "dev"), None),
        P(("grp", "dev"), None),
        P(("grp", "dev"), None),
        P(("grp", "dev")),
        P(("grp", "dev"), None),
        P(),
        P(),
        P(),
        P(),
        P(),
        P(),
        P(),
        P(),
        P(),
        P(),
        P(),
        P(),
    )
    out_specs = (P(("grp", "dev"), None), P(("grp", "dev"), None))
    return jax.shard_map(local, mesh=mesh, in_specs=in_specs, out_specs=out_specs, check_vma=False)
```

```python
import math

import jax
import jax.numpy as jnp
from jax import lax
from jax.experimental import pallas as pl
from jax.experimental.pallas import tpu as pltpu
from jax.sharding import PartitionSpec as P

HEADS = 2
K = 10
CAP_E = 2
CAP_N = 16
CAP = 88
LANES = 128
SHIFT = 65536


def hot(index, size, axis):
    index = jnp.expand_dims(index, axis)
    grid = lax.broadcasted_iota(jnp.int32, index.shape[:axis] + (size,) + index.shape[axis + 1 :], axis)
    return (index == grid).astype(jnp.bfloat16)


def pick(index, table):
    return jnp.dot(hot(index, table.shape[0], 1), table, preferred_element_type=jnp.float32).astype(
        jnp.bfloat16
    )


def split_slot(value, members, slots):
    width = slots.bit_length() - 1
    owner = value >> width
    return owner & (members - 1), ((owner >> (members.bit_length() - 1)) << width) | (value & (slots - 1))


def exchange(x, axis):
    return lax.all_to_all(x, axis, split_axis=0, concat_axis=0, tiled=True)


def event_block(
    end_rows,
    near_rows,
    elapsed,
    near_count,
    frequency,
    phases,
    query_weight,
    key_weight,
    value_weight,
    out_weight,
    out_bias,
    message_in,
    message_out,
):
    events = end_rows.shape[1]
    row_width = end_rows.shape[-1]
    head_size = row_width // HEADS
    fixed_code = jnp.broadcast_to(
        jnp.cos(phases).astype(jnp.bfloat16), (2, events, phases.shape[0])
    )
    near_code = jnp.cos(elapsed[..., None] * frequency + phases).astype(jnp.bfloat16)
    query_in = jnp.concatenate([end_rows, fixed_code], -1)
    queries = jnp.einsum("jec,cd->jed", query_in, query_weight, preferred_element_type=jnp.float32)
    near_in = jnp.concatenate([near_rows, near_code], -1)
    key_rows = jnp.einsum("jkec,cd->jked", near_in, key_weight, preferred_element_type=jnp.float32)
    values = jnp.einsum("jkec,cd->jked", near_in, value_weight, preferred_element_type=jnp.float32)
    usable = jnp.arange(K)[None, :, None] < near_count[:, None, :]
    pieces = []
    for head in range(HEADS):
        low = head * head_size
        high = low + head_size
        scores = jnp.sum(
            queries[:, None, :, low:high] * key_rows[..., low:high], axis=-1
        ) / math.sqrt(head_size)
        exponent = jnp.where(usable, jnp.exp(scores), jnp.zeros_like(scores))
        weight = exponent / jnp.sum(exponent, axis=1, keepdims=True)
        pieces.append(jnp.sum(weight[..., None] * values[..., low:high], axis=1))
    attended = jnp.concatenate(pieces, -1).astype(jnp.bfloat16)
    joined = jnp.concatenate([attended, end_rows], -1)
    embedded = jax.nn.relu(
        jnp.einsum("jec,cd->jed", joined, out_weight, preferred_element_type=jnp.float32) + out_bias
    ).astype(jnp.bfloat16)
    paired = jnp.concatenate([embedded, embedded[::-1]], -1)
    hidden = jax.nn.relu(
        jnp.einsum("jec,cd->jed", paired, message_in, preferred_element_type=jnp.float32)
    ).astype(jnp.bfloat16)
    message = jnp.einsum("jec,cd->jed", hidden, message_out, preferred_element_type=jnp.float32)
    return (embedded, message)


def across(left, right):
    return lax.dot_general(
        left, right, (((1,), (1,)), ((), ())), preferred_element_type=jnp.float32
    )


def request_kernel(mine, near_slot, end_slot, count, want_end, want_near, first, rank_or_none):
    groups = first.shape[0]
    members, places = rank_or_none.shape
    events = near_slot.shape[1]
    owners = groups * members
    block = groups * CAP_N

    def ones(match):
        return jnp.where(match, 1.0, 0.0).astype(jnp.bfloat16)

    def numbers(size, width):
        return lax.broadcasted_iota(jnp.int32, (size, width), 0)

    def lanes(size, width):
        return lax.broadcasted_iota(jnp.int32, (size, width), 1)

    member_pieces = []
    place_pieces = []
    for line in range(2 * K):
        member, place = split_slot(near_slot[line : line + 1, :], members, CAP_N)
        side = line // K
        member = jnp.where(line - side * K < count[side : side + 1, :], member, -1)
        member_pieces.append(ones(numbers(members, events) == member))
        place_pieces.append(ones(numbers(places, events) == place))
    group_pieces = []
    lane_pieces = []
    for line in range(2):
        value = end_slot[line : line + 1, :]
        member, place = split_slot(value, members, CAP_E)
        member_pieces.append(ones(numbers(members, events) == member))
        place_pieces.append(ones(numbers(places, events) == place + block))
        group = value >> (CAP_E * members).bit_length() - 1
        group_pieces.append(ones(numbers(groups, events) == group))
        lane_pieces.append(ones(numbers(LANES, events) == (value & (CAP_E - 1)) * members + member))
    uses = across(jnp.concatenate(member_pieces, 1), jnp.concatenate(place_pieces, 1))
    used = ones(uses > 0)
    before = ones(numbers(places, places) < lanes(places, places))
    rank = jnp.dot(used, before, preferred_element_type=jnp.float32)
    rank_or_none[...] = jnp.where(uses > 0, rank, -1.0).astype(jnp.int32)
    most = jnp.max(jnp.sum(used.astype(jnp.float32), axis=1, keepdims=True)).astype(jnp.int32)
    times = across(jnp.concatenate(group_pieces, 1), jnp.concatenate(lane_pieces, 1)).astype(jnp.int32)

    group = lanes(groups, owners) >> members.bit_length() - 1
    own = group == numbers(groups, owners)
    column = numbers(LANES, owners)
    owner = lanes(LANES, owners)

    def spread(part):
        total = jnp.zeros((groups, LANES), jnp.float32)
        for slot in range(CAP_E):
            row = part(want_end[slot : slot + 1, :])
            total = total + across(
                jnp.where(own, row, 0.0).astype(jnp.bfloat16),
                ones(column == slot * members + (owner & (members - 1))),
            )
        asked = jnp.concatenate(
            [
                jnp.zeros((members * CAP_E, owners), jnp.float32),
                part(want_near[...]),
                jnp.zeros((LANES - members * CAP_E - CAP_N, owners), jnp.float32),
            ],
            0,
        )
        return total + across(
            ones(own & ((lanes(groups, owners) & (members - 1)) == mine[0])),
            asked.astype(jnp.bfloat16),
        )

    high = spread(lambda wanted: ((wanted + 1) >> 4).astype(jnp.float32))
    low = spread(lambda wanted: ((wanted + 1) & 15).astype(jnp.float32))
    wanted = (16 * high + low).astype(jnp.int32) - 1
    lane = lanes(groups, LANES)
    wanted = jnp.where((lane < members * CAP_E) & (wanted >= 0), wanted + SHIFT * times, wanted)
    first[...] = jnp.where(lane < members * CAP_E + CAP_N, wanted, most)


def event_kernel(
    lanes,
    table,
    count,
    slot,
    code,
    fixed,
    query_weight,
    pair_weight,
    out_weight,
    out_bias,
    message_in,
    message_out,
    embedded,
    slot_sum,
    halves,
    even_left,
    even_right,
    odd_left,
    odd_right,
    values,
    exponents,
):
    rows, width = table.shape
    pairs = count.shape[1]
    events = pairs // 2
    head_size = width // HEADS
    one = jnp.bfloat16(1)
    none = jnp.bfloat16(0)

    def dot(left, right):
        return jnp.dot(left, right, preferred_element_type=jnp.float32)

    def near(index, first, size):
        return jnp.clip(index - first, -1, size).astype(jnp.float32).astype(jnp.bfloat16)

    row = lax.broadcasted_iota(jnp.int32, (width, width), 0)
    column = lax.broadcasted_iota(jnp.int32, (width, width), 1)
    unit = jnp.where(row == column, 1.0, 0.0).astype(jnp.bfloat16)
    for low in range(0, rows, width):
        part = table[low : low + width, :].astype(jnp.float32)
        halves[0, low : low + width, :] = part[:, :LANES]
        halves[1, low : low + width, :] = part[:, LANES:]

    def fetch(line, left, right):
        for lane in range(pairs):
            index = lanes[line * pairs + lane]
            left[lane : lane + 1, :] = halves[0, pl.ds(index, 1), :]
            right[lane : lane + 1, :] = halves[1, pl.ds(index, 1), :]

    def fetched(left, right):
        return jnp.concatenate(
            [left[...].astype(jnp.bfloat16), right[...].astype(jnp.bfloat16)], 1
        )

    fetch(K, odd_left, odd_right)
    fetch(0, even_left, even_right)
    end_rows = fetched(odd_left, odd_right)
    ends = across(unit, end_rows).astype(jnp.bfloat16)
    queries = dot(query_weight[:, :width], ends) + across(
        query_weight[:, width:], jnp.broadcast_to(fixed[...], (pairs, fixed.shape[1]))
    )

    def neighbour(k, left, right):
        pair = across(pair_weight[:, :width], fetched(left, right)) + dot(
            pair_weight[:, width:], code[k]
        )
        values[k] = pair[width:]
        product = queries * pair[:width]
        for head in range(HEADS):
            scores = jnp.sum(
                product[head * head_size : (head + 1) * head_size], axis=0, keepdims=True
            ) / math.sqrt(head_size)
            exponents[k, head : head + 1, :] = jnp.where(k < count[...], jnp.exp(scores), 0.0)

    def two(step, carry):
        k = 2 * step
        fetch(k + 1, odd_left, odd_right)
        neighbour(k, even_left, even_right)
        fetch(k + 2, even_left, even_right)
        neighbour(k + 1, odd_left, odd_right)
        return carry

    lax.fori_loop(0, K // 2, two, 0)
    pieces = []
    for head in range(HEADS):
        low = head * head_size
        high = low + head_size
        total = exponents[0, head : head + 1, :]
        for k in range(1, K):
            total = total + exponents[k, head : head + 1, :]
        piece = jnp.zeros((head_size, pairs), jnp.float32)
        for k in range(K):
            piece = piece + exponents[k, head : head + 1, :] / total * values[k, low:high, :]
        pieces.append(piece)
    attended = jnp.concatenate(pieces, 0).astype(jnp.bfloat16)
    embeds = jnp.maximum(
        dot(out_weight[:, :width], attended)
        + dot(out_weight[:, width:], ends)
        + jnp.transpose(jnp.broadcast_to(out_bias[...], (pairs, width))),
        0.0,
    ).astype(jnp.bfloat16)
    other = jnp.concatenate([embeds[:, events:], embeds[:, :events]], 1)
    hidden = jnp.maximum(
        dot(message_in[:, :width], embeds) + dot(message_in[:, width:], other), 0.0
    ).astype(jnp.bfloat16)
    message = dot(message_out[...], hidden)
    numbers = lax.broadcasted_iota(jnp.int32, (width, pairs), 0).astype(jnp.float32)
    numbers = numbers.astype(jnp.bfloat16)
    high = message.astype(jnp.bfloat16)
    low = (message - high.astype(jnp.float32)).astype(jnp.bfloat16)
    for first in range(0, slot_sum.shape[0], width):
        chosen = jnp.where(numbers == near(slot[...], first, width), one, none)
        slot_sum[first : first + width, :] = (across(chosen, high) + across(chosen, low)).astype(
            jnp.bfloat16
        )
    for side in range(2):
        half = embeds[:, side * events : (side + 1) * events]
        embedded[:, side * width : (side + 1) * width] = across(
            unit[:events, :events], half
        ).astype(jnp.bfloat16)


def gru_kernel(news, owned, counts, memory, from_state, input_weight, bias, new_memory):
    nodes, width = memory.shape
    one = jnp.bfloat16(1)
    none = jnp.bfloat16(0)
    size = 128
    numbers = lax.broadcasted_iota(jnp.int32, (size, owned.shape[1]), 0).astype(jnp.float32)
    numbers = numbers.astype(jnp.bfloat16)
    for low in range(0, nodes, size):
        here = slice(low, low + size)
        index = jnp.clip(owned[...] - low, -1, size).astype(jnp.float32).astype(jnp.bfloat16)
        totals = jnp.dot(
            jnp.where(numbers == index, one, none), news[...], preferred_element_type=jnp.float32
        )
        count = jnp.concatenate([counts[here, :]] * (width // LANES), 1)
        averaged = (totals / jnp.maximum(count, 1.0)).astype(jnp.bfloat16)
        from_msg = jnp.dot(averaged, input_weight[...], preferred_element_type=jnp.float32)
        update, reset, last = (slice(i * width, (i + 1) * width) for i in range(3))
        update_gate = jax.nn.sigmoid(from_msg[:, update] + from_state[here, update] + bias[:, update])
        reset_gate = jax.nn.sigmoid(from_msg[:, reset] + from_state[here, reset] + bias[:, reset])
        candidate = jnp.tanh(
            from_msg[:, last] + bias[:, last] + reset_gate * from_state[here, last]
        )
        updated = (1.0 - update_gate) * candidate + update_gate * memory[here, :]
        new_memory[here, :] = jnp.where(count > 0, updated, memory[here, :])


def local(
    memory,
    want_end,
    want_near,
    end_slot,
    near_slot,
    near_count,
    event_time,
    near_time,
    frequency,
    phases,
    query_weight,
    key_weight,
    value_weight,
    out_weight,
    out_bias,
    message_in,
    message_out,
    input_weight,
    state_weight,
    update_bias,
):
    groups = lax.axis_size("grp")
    members = lax.axis_size("dev")
    nodes, row_width = memory.shape
    events = end_slot.shape[0]
    block = groups * CAP_N
    ends = groups * CAP_E
    places = block + ends
    mem_half = memory.astype(jnp.bfloat16)
    counted = jnp.transpose(near_count)

    near_value = jnp.transpose(near_slot)
    end_value = jnp.transpose(end_slot)
    first, rank_or_none = pl.pallas_call(
        request_kernel,
        out_shape=(
            jax.ShapeDtypeStruct((groups, LANES), jnp.int32),
            jax.ShapeDtypeStruct((members, places), jnp.int32),
        ),
        in_specs=[pl.BlockSpec(memory_space=pltpu.SMEM)]
        + [pl.BlockSpec(memory_space=pltpu.VMEM)] * 5,
        name="request_kernel",
    )(
        lax.axis_index("dev").reshape(1),
        near_value,
        end_value,
        counted,
        jnp.transpose(want_end.reshape(-1, CAP_E)),
        jnp.transpose(want_near.reshape(-1, CAP_N)),
    )
    first = exchange(first, "grp")

    near_value = near_value.reshape(-1)
    end_value = end_value.reshape(-1)
    near_member, near_place = split_slot(near_value, members, CAP_N)
    end_member, end_place = split_slot(end_value, members, CAP_E)
    usable = (jnp.arange(K)[None, :, None] < counted[:, None, :]).reshape(-1)
    member = jnp.concatenate([jnp.where(usable, near_member, -1), end_member])
    place = jnp.concatenate([near_place, end_place + block])
    listed = jnp.sum(
        jnp.where(
            rank_or_none[:, None, :] == jnp.arange(CAP)[None, :, None],
            jnp.arange(places)[None, None, :],
            0,
        ),
        axis=2,
    )
    ref_rank = jnp.sum(
        jnp.dot(
            jnp.minimum(rank_or_none, CAP).astype(jnp.bfloat16),
            hot(place, places, 0),
            preferred_element_type=jnp.float32,
        )
        * hot(member, members, 0).astype(jnp.float32),
        axis=0,
    ).astype(jnp.int32)
    index = jnp.where(member >= 0, member * CAP + jnp.minimum(ref_rank, CAP - 1), 0)

    got_near = first[:, members * CAP_E : members * CAP_E + CAP_N]
    most = jnp.max(first[:, members * CAP_E + CAP_N :])
    passed = jnp.transpose(
        first[:, : members * CAP_E].reshape(groups, CAP_E, members), (2, 0, 1)
    ).reshape(members, ends)
    second = jnp.concatenate(
        [
            passed,
            listed,
            jnp.broadcast_to(most, (members, LANES - ends - CAP)),
        ],
        1,
    )
    second = exchange(second, "dev")
    got_listed = second[:, ends : ends + CAP]
    most = jnp.max(second[:, ends + CAP :])
    got_code = second[:, :ends].reshape(members, groups, CAP_E)
    got_code = jnp.transpose(got_code, (1, 0, 2)).reshape(groups, members * CAP_E)
    got_end = jnp.where(got_code >= 0, got_code & (SHIFT - 1), -1)
    got_count = jnp.where(got_code >= 0, got_code >> 16, 0)

    row_index = jnp.concatenate([got_near, got_end], 1).reshape(-1)
    rows = exchange(pick(row_index, mem_half).reshape(groups, -1, row_width), "grp")
    near_block = rows[:, :CAP_N].reshape(block, row_width)
    end_part = jnp.transpose(
        rows[:, CAP_N:].reshape(groups, members, CAP_E, row_width), (1, 0, 2, 3)
    ).reshape(members, ends, row_width)
    near_part = jnp.dot(
        hot(got_listed.reshape(-1), block, 1), near_block, preferred_element_type=jnp.float32
    ).reshape(members, CAP, row_width)
    listed_ends = jnp.einsum(
        "dcp,dpw->dcw",
        hot(got_listed - block, ends, 2),
        end_part,
        preferred_element_type=jnp.float32,
    )
    table = exchange((near_part + listed_ends).astype(jnp.bfloat16), "dev")
    table = table.reshape(members * CAP, row_width)

    elapsed = (event_time[None, :] - jnp.transpose(near_time)).astype(jnp.float32)
    elapsed = elapsed.reshape(2, K, events)

    def by_owner(sums):
        return sums.reshape(groups * members, CAP_E, row_width)

    def whole():
        full = jnp.broadcast_to(near_block[None], (members, block, row_width))
        full = exchange(jnp.concatenate([full, end_part], 1), "dev")
        fetched = jnp.take(
            full.reshape(members * places, row_width),
            jnp.where(member >= 0, member * places + place, 0),
            axis=0,
            mode="clip",
        )
        embedded, message = event_block(
            fetched[2 * K * events :].reshape(2, events, row_width),
            fetched[: 2 * K * events].reshape(2, K, events, row_width),
            elapsed,
            counted,
            frequency,
            phases,
            query_weight,
            key_weight,
            value_weight,
            out_weight,
            out_bias,
            message_in,
            message_out,
        )
        message = message.reshape(-1, row_width)
        high = lax.reduce_precision(message, 8, 7)
        end_hot = hot(end_value, groups * members * CAP_E, 0)
        slot_sum = jnp.dot(
            end_hot, high.astype(jnp.bfloat16), preferred_element_type=jnp.float32
        ) + jnp.dot(
            end_hot, (message - high).astype(jnp.bfloat16), preferred_element_type=jnp.float32
        )
        return jnp.concatenate([embedded[0], embedded[1]], 1), by_owner(slot_sum.astype(jnp.bfloat16))

    pairs = 2 * events
    near_lanes = jnp.transpose(index[: 2 * K * events].reshape(2, K, events), (1, 0, 2))
    lanes = jnp.concatenate([near_lanes.reshape(-1), index[2 * K * events :]])
    elapsed_lanes = jnp.transpose(elapsed, (1, 0, 2)).reshape(K, 1, pairs)
    code = jnp.cos(elapsed_lanes * frequency[None, :, None] + phases[None, :, None])
    fixed = jnp.cos(phases)[None, :]
    operands = (
        counted.reshape(1, pairs),
        end_value.reshape(1, pairs),
        code.astype(jnp.bfloat16),
        fixed.astype(jnp.bfloat16),
        jnp.transpose(query_weight),
        jnp.transpose(jnp.concatenate([key_weight, value_weight], 1)),
        jnp.transpose(out_weight),
        out_bias[None, :],
        jnp.transpose(message_in),
        jnp.transpose(message_out),
    )

    def listed_only():
        embedded, slot_sum = pl.pallas_call(
            event_kernel,
            out_shape=(
                jax.ShapeDtypeStruct((events, 2 * row_width), jnp.bfloat16),
                jax.ShapeDtypeStruct((groups * members * CAP_E, row_width), jnp.bfloat16),
            ),
            in_specs=[pl.BlockSpec(memory_space=pltpu.SMEM)]
            + [pl.BlockSpec(memory_space=pltpu.VMEM)] * (1 + len(operands)),
            scratch_shapes=[pltpu.VMEM((row_width // LANES, table.shape[0], LANES), jnp.float32)]
            + [pltpu.VMEM((pairs, LANES), jnp.float32)] * 4
            + [
                pltpu.VMEM((K, row_width, pairs), jnp.float32),
                pltpu.VMEM((K, 8, pairs), jnp.float32),
            ],
            name="event_kernel",
        )(lanes, table, *operands)
        return embedded, by_owner(slot_sum)

    embedded, slot_sum = lax.cond(most > CAP, whole, listed_only)
    news = exchange(
        slot_sum, ("grp", "dev")
    ).reshape(-1, row_width)
    owned = got_end.reshape(-1)
    counts = jnp.sum(
        jnp.where(
            owned[None, :] == jnp.arange(nodes)[:, None], got_count.reshape(1, -1), 0
        ),
        axis=1,
    ).astype(jnp.float32)
    new_memory = pl.pallas_call(
        gru_kernel,
        out_shape=jax.ShapeDtypeStruct(memory.shape, memory.dtype),
        name="gru_kernel",
    )(
        news,
        owned[None, :],
        jnp.broadcast_to(counts[:, None], (nodes, LANES)),
        memory,
        jnp.dot(mem_half, state_weight, preferred_element_type=jnp.float32),
        input_weight,
        update_bias[None, :],
    )
    return (new_memory, embedded)


def solution(mesh):
    in_specs = (
        P(("grp", "dev"), None),
        P(("grp", "dev"), None, None),
        P(("grp", "dev"), None, None),
        P(("grp", "dev"), None),
        P(("grp", "dev"), None),
        P(("grp", "dev"), None),
        P(("grp", "dev")),
        P(("grp", "dev"), None),
        P(),
        P(),
        P(),
        P(),
        P(),
        P(),
        P(),
        P(),
        P(),
        P(),
        P(),
        P(),
    )
    out_specs = (P(("grp", "dev"), None), P(("grp", "dev"), None))
    return jax.shard_map(local, mesh=mesh, in_specs=in_specs, out_specs=out_specs, check_vma=False)
```

```python
import math

import jax
import jax.numpy as jnp
from jax import lax
from jax.experimental import pallas as pl
from jax.experimental.pallas import tpu as pltpu
from jax.sharding import PartitionSpec as P

HEADS = 2
K = 10
CAP_E = 2
CAP_N = 16
CAP = 88
LANES = 128
SHIFT = 65536


def hot(index, size, axis):
    index = jnp.expand_dims(index, axis)
    grid = lax.broadcasted_iota(jnp.int32, index.shape[:axis] + (size,) + index.shape[axis + 1 :], axis)
    return (index == grid).astype(jnp.bfloat16)


def pick(index, table):
    return jnp.dot(hot(index, table.shape[0], 1), table, preferred_element_type=jnp.float32).astype(
        jnp.bfloat16
    )


def split_slot(value, members, slots):
    width = slots.bit_length() - 1
    owner = value >> width
    return owner & (members - 1), ((owner >> (members.bit_length() - 1)) << width) | (value & (slots - 1))


def exchange(x, axis):
    return lax.all_to_all(x, axis, split_axis=0, concat_axis=0, tiled=True)


def event_block(
    end_rows,
    near_rows,
    elapsed,
    near_count,
    frequency,
    phases,
    query_weight,
    key_weight,
    value_weight,
    out_weight,
    out_bias,
    message_in,
    message_out,
):
    events = end_rows.shape[1]
    row_width = end_rows.shape[-1]
    head_size = row_width // HEADS
    fixed_code = jnp.broadcast_to(
        jnp.cos(phases).astype(jnp.bfloat16), (2, events, phases.shape[0])
    )
    near_code = jnp.cos(elapsed[..., None] * frequency + phases).astype(jnp.bfloat16)
    query_in = jnp.concatenate([end_rows, fixed_code], -1)
    queries = jnp.einsum("jec,cd->jed", query_in, query_weight, preferred_element_type=jnp.float32)
    near_in = jnp.concatenate([near_rows, near_code], -1)
    key_rows = jnp.einsum("jkec,cd->jked", near_in, key_weight, preferred_element_type=jnp.float32)
    values = jnp.einsum("jkec,cd->jked", near_in, value_weight, preferred_element_type=jnp.float32)
    usable = jnp.arange(K)[None, :, None] < near_count[:, None, :]
    pieces = []
    for head in range(HEADS):
        low = head * head_size
        high = low + head_size
        scores = jnp.sum(
            queries[:, None, :, low:high] * key_rows[..., low:high], axis=-1
        ) / math.sqrt(head_size)
        exponent = jnp.where(usable, jnp.exp(scores), jnp.zeros_like(scores))
        weight = exponent / jnp.sum(exponent, axis=1, keepdims=True)
        pieces.append(jnp.sum(weight[..., None] * values[..., low:high], axis=1))
    attended = jnp.concatenate(pieces, -1).astype(jnp.bfloat16)
    joined = jnp.concatenate([attended, end_rows], -1)
    embedded = jax.nn.relu(
        jnp.einsum("jec,cd->jed", joined, out_weight, preferred_element_type=jnp.float32) + out_bias
    ).astype(jnp.bfloat16)
    paired = jnp.concatenate([embedded, embedded[::-1]], -1)
    hidden = jax.nn.relu(
        jnp.einsum("jec,cd->jed", paired, message_in, preferred_element_type=jnp.float32)
    ).astype(jnp.bfloat16)
    message = jnp.einsum("jec,cd->jed", hidden, message_out, preferred_element_type=jnp.float32)
    return (embedded, message)


def across(left, right):
    return lax.dot_general(
        left, right, (((1,), (1,)), ((), ())), preferred_element_type=jnp.float32
    )


def request_kernel(mine, near_slot, end_slot, count, want_end, want_near, first, rank_or_none):
    groups = first.shape[0]
    members, places = rank_or_none.shape
    events = near_slot.shape[1]
    owners = groups * members
    block = groups * CAP_N

    def ones(match):
        return jnp.where(match, 1.0, 0.0).astype(jnp.bfloat16)

    def numbers(size, width):
        return lax.broadcasted_iota(jnp.int32, (size, width), 0)

    def lanes(size, width):
        return lax.broadcasted_iota(jnp.int32, (size, width), 1)

    member_pieces = []
    place_pieces = []
    for line in range(2 * K):
        member, place = split_slot(near_slot[line : line + 1, :], members, CAP_N)
        side = line // K
        member = jnp.where(line - side * K < count[side : side + 1, :], member, -1)
        member_pieces.append(ones(numbers(members, events) == member))
        place_pieces.append(ones(numbers(places, events) == place))
    group_pieces = []
    lane_pieces = []
    for line in range(2):
        value = end_slot[line : line + 1, :]
        member, place = split_slot(value, members, CAP_E)
        member_pieces.append(ones(numbers(members, events) == member))
        place_pieces.append(ones(numbers(places, events) == place + block))
        group = value >> (CAP_E * members).bit_length() - 1
        group_pieces.append(ones(numbers(groups, events) == group))
        lane_pieces.append(ones(numbers(LANES, events) == (value & (CAP_E - 1)) * members + member))
    uses = across(jnp.concatenate(member_pieces, 1), jnp.concatenate(place_pieces, 1))
    used = ones(uses > 0)
    before = ones(numbers(places, places) < lanes(places, places))
    rank = jnp.dot(used, before, preferred_element_type=jnp.float32)
    rank_or_none[...] = jnp.where(uses > 0, rank, -1.0).astype(jnp.int32)
    most = jnp.max(jnp.sum(used.astype(jnp.float32), axis=1, keepdims=True)).astype(jnp.int32)
    times = across(jnp.concatenate(group_pieces, 1), jnp.concatenate(lane_pieces, 1)).astype(jnp.int32)

    group = lanes(groups, owners) >> members.bit_length() - 1
    own = group == numbers(groups, owners)
    column = numbers(LANES, owners)
    owner = lanes(LANES, owners)

    def spread(part):
        total = jnp.zeros((groups, LANES), jnp.float32)
        for slot in range(CAP_E):
            row = part(want_end[slot : slot + 1, :])
            total = total + across(
                jnp.where(own, row, 0.0).astype(jnp.bfloat16),
                ones(column == slot * members + (owner & (members - 1))),
            )
        asked = jnp.concatenate(
            [
                jnp.zeros((members * CAP_E, owners), jnp.float32),
                part(want_near[...]),
                jnp.zeros((LANES - members * CAP_E - CAP_N, owners), jnp.float32),
            ],
            0,
        )
        return total + across(
            ones(own & ((lanes(groups, owners) & (members - 1)) == mine[0])),
            asked.astype(jnp.bfloat16),
        )

    high = spread(lambda wanted: ((wanted + 1) >> 4).astype(jnp.float32))
    low = spread(lambda wanted: ((wanted + 1) & 15).astype(jnp.float32))
    wanted = (16 * high + low).astype(jnp.int32) - 1
    lane = lanes(groups, LANES)
    wanted = jnp.where((lane < members * CAP_E) & (wanted >= 0), wanted + SHIFT * times, wanted)
    first[...] = jnp.where(lane < members * CAP_E + CAP_N, wanted, most)


def event_kernel(
    lanes,
    table,
    count,
    slot,
    code,
    fixed,
    query_weight,
    pair_weight,
    out_weight,
    out_bias,
    message_in,
    message_out,
    embedded,
    slot_sum,
    halves,
    even_left,
    even_right,
    odd_left,
    odd_right,
    values,
    exponents,
):
    rows, width = table.shape
    pairs = count.shape[1]
    events = pairs // 2
    head_size = width // HEADS
    one = jnp.bfloat16(1)
    none = jnp.bfloat16(0)

    def dot(left, right):
        return jnp.dot(left, right, preferred_element_type=jnp.float32)

    def near(index, first, size):
        return jnp.clip(index - first, -1, size).astype(jnp.float32).astype(jnp.bfloat16)

    row = lax.broadcasted_iota(jnp.int32, (width, width), 0)
    column = lax.broadcasted_iota(jnp.int32, (width, width), 1)
    unit = jnp.where(row == column, 1.0, 0.0).astype(jnp.bfloat16)
    for low in range(0, rows, width):
        part = table[low : low + width, :].astype(jnp.float32)
        halves[0, low : low + width, :] = part[:, :LANES]
        halves[1, low : low + width, :] = part[:, LANES:]

    def fetch(line, left, right):
        for lane in range(pairs):
            index = lanes[line * pairs + lane]
            left[lane : lane + 1, :] = halves[0, pl.ds(index, 1), :]
            right[lane : lane + 1, :] = halves[1, pl.ds(index, 1), :]

    def fetched(left, right):
        return jnp.concatenate(
            [left[...].astype(jnp.bfloat16), right[...].astype(jnp.bfloat16)], 1
        )

    fetch(K, odd_left, odd_right)
    fetch(0, even_left, even_right)
    end_rows = fetched(odd_left, odd_right)
    ends = across(unit, end_rows).astype(jnp.bfloat16)
    queries = dot(query_weight[:, :width], ends) + across(
        query_weight[:, width:], jnp.broadcast_to(fixed[...], (pairs, fixed.shape[1]))
    )

    def neighbour(k, left, right):
        pair = across(pair_weight[:, :width], fetched(left, right)) + dot(
            pair_weight[:, width:], code[k]
        )
        values[k] = pair[width:]
        product = queries * pair[:width]
        for head in range(HEADS):
            scores = jnp.sum(
                product[head * head_size : (head + 1) * head_size], axis=0, keepdims=True
            ) / math.sqrt(head_size)
            exponents[k, head : head + 1, :] = jnp.where(k < count[...], jnp.exp(scores), 0.0)

    def two(step, carry):
        k = 2 * step
        fetch(k + 1, odd_left, odd_right)
        neighbour(k, even_left, even_right)
        fetch(k + 2, even_left, even_right)
        neighbour(k + 1, odd_left, odd_right)
        return carry

    lax.fori_loop(0, K // 2, two, 0)
    pieces = []
    for head in range(HEADS):
        low = head * head_size
        high = low + head_size
        total = exponents[0, head : head + 1, :]
        for k in range(1, K):
            total = total + exponents[k, head : head + 1, :]
        piece = jnp.zeros((head_size, pairs), jnp.float32)
        for k in range(K):
            piece = piece + exponents[k, head : head + 1, :] / total * values[k, low:high, :]
        pieces.append(piece)
    attended = jnp.concatenate(pieces, 0).astype(jnp.bfloat16)
    embeds = jnp.maximum(
        dot(out_weight[:, :width], attended)
        + dot(out_weight[:, width:], ends)
        + jnp.transpose(jnp.broadcast_to(out_bias[...], (pairs, width))),
        0.0,
    ).astype(jnp.bfloat16)
    other = jnp.concatenate([embeds[:, events:], embeds[:, :events]], 1)
    hidden = jnp.maximum(
        dot(message_in[:, :width], embeds) + dot(message_in[:, width:], other), 0.0
    ).astype(jnp.bfloat16)
    message = dot(message_out[...], hidden)
    numbers = lax.broadcasted_iota(jnp.int32, (width, pairs), 0).astype(jnp.float32)
    numbers = numbers.astype(jnp.bfloat16)
    high = message.astype(jnp.bfloat16)
    low = (message - high.astype(jnp.float32)).astype(jnp.bfloat16)
    for first in range(0, slot_sum.shape[0], width):
        chosen = jnp.where(numbers == near(slot[...], first, width), one, none)
        slot_sum[first : first + width, :] = (across(chosen, high) + across(chosen, low)).astype(
            jnp.bfloat16
        )
    for side in range(2):
        half = embeds[:, side * events : (side + 1) * events]
        embedded[:, side * width : (side + 1) * width] = across(
            unit[:events, :events], half
        ).astype(jnp.bfloat16)


def gru_kernel(news, owned, times, memory, from_state, input_weight, bias, new_memory):
    nodes, width = memory.shape
    low = pl.program_id(0) * nodes
    numbers = lax.broadcasted_iota(jnp.int32, (nodes, owned.shape[1]), 0).astype(jnp.float32)
    index = jnp.clip(owned[...] - low, -1, nodes).astype(jnp.float32).astype(jnp.bfloat16)
    chosen = jnp.where(numbers.astype(jnp.bfloat16) == index, jnp.bfloat16(1), jnp.bfloat16(0))
    totals = jnp.dot(chosen, news[...], preferred_element_type=jnp.float32)
    repeated = jnp.broadcast_to(times[...].astype(jnp.float32), (LANES, times.shape[1]))
    count = across(chosen, repeated.astype(jnp.bfloat16))
    count = jnp.concatenate([count] * (width // LANES), 1)
    averaged = (totals / jnp.maximum(count, 1.0)).astype(jnp.bfloat16)
    from_msg = jnp.dot(averaged, input_weight[...], preferred_element_type=jnp.float32)
    update, reset, last = (slice(i * width, (i + 1) * width) for i in range(3))
    update_gate = jax.nn.sigmoid(from_msg[:, update] + from_state[:, update] + bias[:, update])
    reset_gate = jax.nn.sigmoid(from_msg[:, reset] + from_state[:, reset] + bias[:, reset])
    candidate = jnp.tanh(from_msg[:, last] + bias[:, last] + reset_gate * from_state[:, last])
    updated = (1.0 - update_gate) * candidate + update_gate * memory[...]
    new_memory[...] = jnp.where(count > 0, updated, memory[...])


def local(
    memory,
    want_end,
    want_near,
    end_slot,
    near_slot,
    near_count,
    event_time,
    near_time,
    frequency,
    phases,
    query_weight,
    key_weight,
    value_weight,
    out_weight,
    out_bias,
    message_in,
    message_out,
    input_weight,
    state_weight,
    update_bias,
):
    groups = lax.axis_size("grp")
    members = lax.axis_size("dev")
    nodes, row_width = memory.shape
    events = end_slot.shape[0]
    block = groups * CAP_N
    ends = groups * CAP_E
    places = block + ends
    mem_half = memory.astype(jnp.bfloat16)
    counted = jnp.transpose(near_count)

    near_value = jnp.transpose(near_slot)
    end_value = jnp.transpose(end_slot)
    first, rank_or_none = pl.pallas_call(
        request_kernel,
        out_shape=(
            jax.ShapeDtypeStruct((groups, LANES), jnp.int32),
            jax.ShapeDtypeStruct((members, places), jnp.int32),
        ),
        in_specs=[pl.BlockSpec(memory_space=pltpu.SMEM)]
        + [pl.BlockSpec(memory_space=pltpu.VMEM)] * 5,
        name="request_kernel",
    )(
        lax.axis_index("dev").reshape(1),
        near_value,
        end_value,
        counted,
        jnp.transpose(want_end.reshape(-1, CAP_E)),
        jnp.transpose(want_near.reshape(-1, CAP_N)),
    )
    first = exchange(first, "grp")

    near_value = near_value.reshape(-1)
    end_value = end_value.reshape(-1)
    near_member, near_place = split_slot(near_value, members, CAP_N)
    end_member, end_place = split_slot(end_value, members, CAP_E)
    usable = (jnp.arange(K)[None, :, None] < counted[:, None, :]).reshape(-1)
    member = jnp.concatenate([jnp.where(usable, near_member, -1), end_member])
    place = jnp.concatenate([near_place, end_place + block])
    listed = jnp.sum(
        jnp.where(
            rank_or_none[:, None, :] == jnp.arange(CAP)[None, :, None],
            jnp.arange(places)[None, None, :],
            0,
        ),
        axis=2,
    )
    ref_rank = jnp.sum(
        jnp.dot(
            jnp.minimum(rank_or_none, CAP).astype(jnp.bfloat16),
            hot(place, places, 0),
            preferred_element_type=jnp.float32,
        )
        * hot(member, members, 0).astype(jnp.float32),
        axis=0,
    ).astype(jnp.int32)
    index = jnp.where(member >= 0, member * CAP + jnp.minimum(ref_rank, CAP - 1), 0)

    got_near = first[:, members * CAP_E : members * CAP_E + CAP_N]
    most = jnp.max(first[:, members * CAP_E + CAP_N :])
    passed = jnp.transpose(
        first[:, : members * CAP_E].reshape(groups, CAP_E, members), (2, 0, 1)
    ).reshape(members, ends)
    second = jnp.concatenate(
        [passed, listed, jnp.zeros((members, LANES - ends - CAP), jnp.int32)], 1
    )
    second = jnp.where(jnp.arange(LANES)[None, :] < ends + CAP, second, most)
    second = exchange(second, "dev")
    got_listed = second[:, ends : ends + CAP]
    most = jnp.max(second[:, ends + CAP :])
    got_code = second[:, :ends].reshape(members, groups, CAP_E)
    got_code = jnp.transpose(got_code, (1, 0, 2)).reshape(groups, members * CAP_E)
    got_end = jnp.where(got_code >= 0, got_code & (SHIFT - 1), -1)
    got_count = jnp.where(got_code >= 0, got_code >> 16, 0)

    row_index = jnp.concatenate([got_near, got_end], 1).reshape(-1)
    rows = exchange(pick(row_index, mem_half).reshape(groups, -1, row_width), "grp")
    near_block = rows[:, :CAP_N].reshape(block, row_width)
    end_part = jnp.transpose(
        rows[:, CAP_N:].reshape(groups, members, CAP_E, row_width), (1, 0, 2, 3)
    ).reshape(members, ends, row_width)
    near_part = jnp.dot(
        hot(got_listed.reshape(-1), block, 1), near_block, preferred_element_type=jnp.float32
    ).reshape(members, CAP, row_width)
    listed_ends = jnp.einsum(
        "dcp,dpw->dcw",
        hot(got_listed - block, ends, 2),
        end_part,
        preferred_element_type=jnp.float32,
    )
    table = exchange((near_part + listed_ends).astype(jnp.bfloat16), "dev")
    table = table.reshape(members * CAP, row_width)

    elapsed = (event_time[None, :] - jnp.transpose(near_time)).astype(jnp.float32)
    elapsed = elapsed.reshape(2, K, events)

    def by_owner(sums):
        return sums.reshape(groups * members, CAP_E, row_width)

    def whole():
        full = jnp.broadcast_to(near_block[None], (members, block, row_width))
        full = exchange(jnp.concatenate([full, end_part], 1), "dev")
        fetched = jnp.take(
            full.reshape(members * places, row_width),
            jnp.where(member >= 0, member * places + place, 0),
            axis=0,
            mode="clip",
        )
        embedded, message = event_block(
            fetched[2 * K * events :].reshape(2, events, row_width),
            fetched[: 2 * K * events].reshape(2, K, events, row_width),
            elapsed,
            counted,
            frequency,
            phases,
            query_weight,
            key_weight,
            value_weight,
            out_weight,
            out_bias,
            message_in,
            message_out,
        )
        message = message.reshape(-1, row_width)
        high = lax.reduce_precision(message, 8, 7)
        end_hot = hot(end_value, groups * members * CAP_E, 0)
        slot_sum = jnp.dot(
            end_hot, high.astype(jnp.bfloat16), preferred_element_type=jnp.float32
        ) + jnp.dot(
            end_hot, (message - high).astype(jnp.bfloat16), preferred_element_type=jnp.float32
        )
        return jnp.concatenate([embedded[0], embedded[1]], 1), by_owner(slot_sum.astype(jnp.bfloat16))

    pairs = 2 * events
    near_lanes = jnp.transpose(index[: 2 * K * events].reshape(2, K, events), (1, 0, 2))
    lanes = jnp.concatenate([near_lanes.reshape(-1), index[2 * K * events :]])
    elapsed_lanes = jnp.transpose(elapsed, (1, 0, 2)).reshape(K, 1, pairs)
    code = jnp.cos(elapsed_lanes * frequency[None, :, None] + phases[None, :, None])
    fixed = jnp.cos(phases)[None, :]
    operands = (
        counted.reshape(1, pairs),
        end_value.reshape(1, pairs),
        code.astype(jnp.bfloat16),
        fixed.astype(jnp.bfloat16),
        jnp.transpose(query_weight),
        jnp.transpose(jnp.concatenate([key_weight, value_weight], 1)),
        jnp.transpose(out_weight),
        out_bias[None, :],
        jnp.transpose(message_in),
        jnp.transpose(message_out),
    )

    def listed_only():
        embedded, slot_sum = pl.pallas_call(
            event_kernel,
            out_shape=(
                jax.ShapeDtypeStruct((events, 2 * row_width), jnp.bfloat16),
                jax.ShapeDtypeStruct((groups * members * CAP_E, row_width), jnp.bfloat16),
            ),
            in_specs=[pl.BlockSpec(memory_space=pltpu.SMEM)]
            + [pl.BlockSpec(memory_space=pltpu.VMEM)] * (1 + len(operands)),
            scratch_shapes=[pltpu.VMEM((row_width // LANES, table.shape[0], LANES), jnp.float32)]
            + [pltpu.VMEM((pairs, LANES), jnp.float32)] * 4
            + [
                pltpu.VMEM((K, row_width, pairs), jnp.float32),
                pltpu.VMEM((K, 8, pairs), jnp.float32),
            ],
            name="event_kernel",
        )(lanes, table, *operands)
        return embedded, by_owner(slot_sum)

    embedded, slot_sum = lax.cond(most > CAP, whole, listed_only)
    news = exchange(
        slot_sum, ("grp", "dev")
    ).reshape(-1, row_width)
    owned = got_end.reshape(-1)
    step = 128
    new_memory = pl.pallas_call(
        gru_kernel,
        grid=(nodes // step,),
        out_shape=jax.ShapeDtypeStruct(memory.shape, memory.dtype),
        in_specs=[
            pl.BlockSpec(news.shape, lambda i: (0, 0)),
            pl.BlockSpec((1, owned.shape[0]), lambda i: (0, 0)),
            pl.BlockSpec((1, owned.shape[0]), lambda i: (0, 0)),
            pl.BlockSpec((step, row_width), lambda i: (i, 0)),
            pl.BlockSpec((step, 3 * row_width), lambda i: (i, 0)),
            pl.BlockSpec(input_weight.shape, lambda i: (0, 0)),
            pl.BlockSpec((1, 3 * row_width), lambda i: (0, 0)),
        ],
        out_specs=pl.BlockSpec((step, row_width), lambda i: (i, 0)),
        name="gru_kernel",
    )(
        news,
        owned[None, :],
        got_count.reshape(1, -1),
        memory,
        jnp.dot(mem_half, state_weight, preferred_element_type=jnp.float32),
        input_weight,
        update_bias[None, :],
    )
    return (new_memory, embedded)


def solution(mesh):
    in_specs = (
        P(("grp", "dev"), None),
        P(("grp", "dev"), None, None),
        P(("grp", "dev"), None, None),
        P(("grp", "dev"), None),
        P(("grp", "dev"), None),
        P(("grp", "dev"), None),
        P(("grp", "dev")),
        P(("grp", "dev"), None),
        P(),
        P(),
        P(),
        P(),
        P(),
        P(),
        P(),
        P(),
        P(),
        P(),
        P(),
        P(),
    )
    out_specs = (P(("grp", "dev"), None), P(("grp", "dev"), None))
    return jax.shard_map(local, mesh=mesh, in_specs=in_specs, out_specs=out_specs, check_vma=False)
```

```python
import math

import jax
import jax.numpy as jnp
from jax import lax
from jax.experimental import pallas as pl
from jax.experimental.pallas import tpu as pltpu
from jax.sharding import PartitionSpec as P

HEADS = 2
K = 10
CAP_E = 2
CAP_N = 16
CAP = 88
LANES = 128
SHIFT = 65536


def hot(index, size, axis):
    index = jnp.expand_dims(index, axis)
    grid = lax.broadcasted_iota(jnp.int32, index.shape[:axis] + (size,) + index.shape[axis + 1 :], axis)
    return (index == grid).astype(jnp.bfloat16)


def pick(index, table):
    return jnp.dot(hot(index, table.shape[0], 1), table, preferred_element_type=jnp.float32).astype(
        jnp.bfloat16
    )


def split_slot(value, members, slots):
    width = slots.bit_length() - 1
    owner = value >> width
    return owner & (members - 1), ((owner >> (members.bit_length() - 1)) << width) | (value & (slots - 1))


def exchange(x, axis):
    return lax.all_to_all(x, axis, split_axis=0, concat_axis=0, tiled=True)


def event_block(
    end_rows,
    near_rows,
    elapsed,
    near_count,
    frequency,
    phases,
    query_weight,
    key_weight,
    value_weight,
    out_weight,
    out_bias,
    message_in,
    message_out,
):
    events = end_rows.shape[1]
    row_width = end_rows.shape[-1]
    head_size = row_width // HEADS
    fixed_code = jnp.broadcast_to(
        jnp.cos(phases).astype(jnp.bfloat16), (2, events, phases.shape[0])
    )
    near_code = jnp.cos(elapsed[..., None] * frequency + phases).astype(jnp.bfloat16)
    query_in = jnp.concatenate([end_rows, fixed_code], -1)
    queries = jnp.einsum("jec,cd->jed", query_in, query_weight, preferred_element_type=jnp.float32)
    near_in = jnp.concatenate([near_rows, near_code], -1)
    key_rows = jnp.einsum("jkec,cd->jked", near_in, key_weight, preferred_element_type=jnp.float32)
    values = jnp.einsum("jkec,cd->jked", near_in, value_weight, preferred_element_type=jnp.float32)
    usable = jnp.arange(K)[None, :, None] < near_count[:, None, :]
    pieces = []
    for head in range(HEADS):
        low = head * head_size
        high = low + head_size
        scores = jnp.sum(
            queries[:, None, :, low:high] * key_rows[..., low:high], axis=-1
        ) / math.sqrt(head_size)
        exponent = jnp.where(usable, jnp.exp(scores), jnp.zeros_like(scores))
        weight = exponent / jnp.sum(exponent, axis=1, keepdims=True)
        pieces.append(jnp.sum(weight[..., None] * values[..., low:high], axis=1))
    attended = jnp.concatenate(pieces, -1).astype(jnp.bfloat16)
    joined = jnp.concatenate([attended, end_rows], -1)
    embedded = jax.nn.relu(
        jnp.einsum("jec,cd->jed", joined, out_weight, preferred_element_type=jnp.float32) + out_bias
    ).astype(jnp.bfloat16)
    paired = jnp.concatenate([embedded, embedded[::-1]], -1)
    hidden = jax.nn.relu(
        jnp.einsum("jec,cd->jed", paired, message_in, preferred_element_type=jnp.float32)
    ).astype(jnp.bfloat16)
    message = jnp.einsum("jec,cd->jed", hidden, message_out, preferred_element_type=jnp.float32)
    return (embedded, message)


def across(left, right):
    return lax.dot_general(
        left, right, (((1,), (1,)), ((), ())), preferred_element_type=jnp.float32
    )


def request_kernel(mine, near_slot, end_slot, count, want_end, want_near, first, rank_or_none):
    groups = first.shape[0]
    members, places = rank_or_none.shape
    events = near_slot.shape[1]
    owners = groups * members
    block = groups * CAP_N

    def ones(match):
        return jnp.where(match, 1.0, 0.0).astype(jnp.bfloat16)

    def numbers(size, width):
        return lax.broadcasted_iota(jnp.int32, (size, width), 0)

    def lanes(size, width):
        return lax.broadcasted_iota(jnp.int32, (size, width), 1)

    member_pieces = []
    place_pieces = []
    for line in range(2 * K):
        member, place = split_slot(near_slot[line : line + 1, :], members, CAP_N)
        side = line // K
        member = jnp.where(line - side * K < count[side : side + 1, :], member, -1)
        member_pieces.append(ones(numbers(members, events) == member))
        place_pieces.append(ones(numbers(places, events) == place))
    group_pieces = []
    lane_pieces = []
    for line in range(2):
        value = end_slot[line : line + 1, :]
        member, place = split_slot(value, members, CAP_E)
        member_pieces.append(ones(numbers(members, events) == member))
        place_pieces.append(ones(numbers(places, events) == place + block))
        group = value >> (CAP_E * members).bit_length() - 1
        group_pieces.append(ones(numbers(groups, events) == group))
        lane_pieces.append(ones(numbers(LANES, events) == (value & (CAP_E - 1)) * members + member))
    uses = across(jnp.concatenate(member_pieces, 1), jnp.concatenate(place_pieces, 1))
    used = ones(uses > 0)
    before = ones(numbers(places, places) < lanes(places, places))
    rank = jnp.dot(used, before, preferred_element_type=jnp.float32)
    rank_or_none[...] = jnp.where(uses > 0, rank, -1.0).astype(jnp.int32)
    most = jnp.max(jnp.sum(used.astype(jnp.float32), axis=1, keepdims=True)).astype(jnp.int32)
    times = across(jnp.concatenate(group_pieces, 1), jnp.concatenate(lane_pieces, 1)).astype(jnp.int32)

    group = lanes(groups, owners) >> members.bit_length() - 1
    own = group == numbers(groups, owners)
    column = numbers(LANES, owners)
    owner = lanes(LANES, owners)

    def spread(part):
        total = jnp.zeros((groups, LANES), jnp.float32)
        for slot in range(CAP_E):
            row = part(want_end[slot : slot + 1, :])
            total = total + across(
                jnp.where(own, row, 0.0).astype(jnp.bfloat16),
                ones(column == slot * members + (owner & (members - 1))),
            )
        asked = jnp.concatenate(
            [
                jnp.zeros((members * CAP_E, owners), jnp.float32),
                part(want_near[...]),
                jnp.zeros((LANES - members * CAP_E - CAP_N, owners), jnp.float32),
            ],
            0,
        )
        return total + across(
            ones(own & ((lanes(groups, owners) & (members - 1)) == mine[0])),
            asked.astype(jnp.bfloat16),
        )

    high = spread(lambda wanted: ((wanted + 1) >> 4).astype(jnp.float32))
    low = spread(lambda wanted: ((wanted + 1) & 15).astype(jnp.float32))
    wanted = (16 * high + low).astype(jnp.int32) - 1
    lane = lanes(groups, LANES)
    wanted = jnp.where((lane < members * CAP_E) & (wanted >= 0), wanted + SHIFT * times, wanted)
    first[...] = jnp.where(lane < members * CAP_E + CAP_N, wanted, most)


def event_kernel(
    lanes,
    table,
    count,
    slot,
    code,
    fixed,
    query_weight,
    pair_weight,
    out_weight,
    out_bias,
    message_in,
    message_out,
    embedded,
    slot_sum,
    halves,
    even_left,
    even_right,
    odd_left,
    odd_right,
    values,
    exponents,
):
    rows, width = table.shape
    pairs = count.shape[1]
    events = pairs // 2
    head_size = width // HEADS
    one = jnp.bfloat16(1)
    none = jnp.bfloat16(0)

    def dot(left, right):
        return jnp.dot(left, right, preferred_element_type=jnp.float32)

    def near(index, first, size):
        return jnp.clip(index - first, -1, size).astype(jnp.float32).astype(jnp.bfloat16)

    row = lax.broadcasted_iota(jnp.int32, (width, width), 0)
    column = lax.broadcasted_iota(jnp.int32, (width, width), 1)
    unit = jnp.where(row == column, 1.0, 0.0).astype(jnp.bfloat16)
    for low in range(0, rows, width):
        part = table[low : low + width, :].astype(jnp.float32)
        halves[0, low : low + width, :] = part[:, :LANES]
        halves[1, low : low + width, :] = part[:, LANES:]

    def fetch(line, left, right):
        for lane in range(pairs):
            index = lanes[line * pairs + lane]
            left[lane : lane + 1, :] = halves[0, pl.ds(index, 1), :]
            right[lane : lane + 1, :] = halves[1, pl.ds(index, 1), :]

    def fetched(left, right):
        return jnp.concatenate(
            [left[...].astype(jnp.bfloat16), right[...].astype(jnp.bfloat16)], 1
        )

    fetch(K, odd_left, odd_right)
    fetch(0, even_left, even_right)
    end_rows = fetched(odd_left, odd_right)
    ends = across(unit, end_rows).astype(jnp.bfloat16)
    queries = dot(query_weight[:, :width], ends) + across(
        query_weight[:, width:], jnp.broadcast_to(fixed[...], (pairs, fixed.shape[1]))
    )

    def neighbour(k, left, right):
        pair = across(pair_weight[:, :width], fetched(left, right)) + dot(
            pair_weight[:, width:], code[k]
        )
        values[k] = pair[width:]
        product = queries * pair[:width]
        for head in range(HEADS):
            scores = jnp.sum(
                product[head * head_size : (head + 1) * head_size], axis=0, keepdims=True
            ) / math.sqrt(head_size)
            exponents[k, head : head + 1, :] = jnp.where(k < count[...], jnp.exp(scores), 0.0)

    def two(step, carry):
        k = 2 * step
        fetch(k + 1, odd_left, odd_right)
        neighbour(k, even_left, even_right)
        fetch(k + 2, even_left, even_right)
        neighbour(k + 1, odd_left, odd_right)
        return carry

    lax.fori_loop(0, K // 2, two, 0)
    pieces = []
    for head in range(HEADS):
        low = head * head_size
        high = low + head_size
        total = exponents[0, head : head + 1, :]
        for k in range(1, K):
            total = total + exponents[k, head : head + 1, :]
        piece = jnp.zeros((head_size, pairs), jnp.float32)
        for k in range(K):
            piece = piece + exponents[k, head : head + 1, :] / total * values[k, low:high, :]
        pieces.append(piece)
    attended = jnp.concatenate(pieces, 0).astype(jnp.bfloat16)
    embeds = jnp.maximum(
        dot(out_weight[:, :width], attended)
        + dot(out_weight[:, width:], ends)
        + jnp.transpose(jnp.broadcast_to(out_bias[...], (pairs, width))),
        0.0,
    ).astype(jnp.bfloat16)
    other = jnp.concatenate([embeds[:, events:], embeds[:, :events]], 1)
    hidden = jnp.maximum(
        dot(message_in[:, :width], embeds) + dot(message_in[:, width:], other), 0.0
    ).astype(jnp.bfloat16)
    message = dot(message_out[...], hidden)
    numbers = lax.broadcasted_iota(jnp.int32, (width, pairs), 0).astype(jnp.float32)
    numbers = numbers.astype(jnp.bfloat16)
    high = message.astype(jnp.bfloat16)
    low = (message - high.astype(jnp.float32)).astype(jnp.bfloat16)
    for first in range(0, slot_sum.shape[0], width):
        chosen = jnp.where(numbers == near(slot[...], first, width), one, none)
        slot_sum[first : first + width, :] = (across(chosen, high) + across(chosen, low)).astype(
            jnp.bfloat16
        )
    for side in range(2):
        half = embeds[:, side * events : (side + 1) * events]
        embedded[:, side * width : (side + 1) * width] = across(
            unit[:events, :events], half
        ).astype(jnp.bfloat16)


def gru_kernel(news, owned, times, memory, from_state, input_weight, bias, new_memory):
    nodes, width = memory.shape
    low = pl.program_id(0) * nodes
    numbers = lax.broadcasted_iota(jnp.int32, (nodes, owned.shape[1]), 0).astype(jnp.float32)
    index = jnp.clip(owned[...] - low, -1, nodes).astype(jnp.float32).astype(jnp.bfloat16)
    chosen = jnp.where(numbers.astype(jnp.bfloat16) == index, jnp.bfloat16(1), jnp.bfloat16(0))
    totals = jnp.dot(chosen, news[...], preferred_element_type=jnp.float32)
    repeated = jnp.broadcast_to(times[...].astype(jnp.float32), (LANES, times.shape[1]))
    count = across(chosen, repeated.astype(jnp.bfloat16))
    count = jnp.concatenate([count] * (width // LANES), 1)
    averaged = (totals / jnp.maximum(count, 1.0)).astype(jnp.bfloat16)
    from_msg = jnp.dot(averaged, input_weight[...], preferred_element_type=jnp.float32)
    update, reset, last = (slice(i * width, (i + 1) * width) for i in range(3))
    update_gate = jax.nn.sigmoid(from_msg[:, update] + from_state[:, update] + bias[:, update])
    reset_gate = jax.nn.sigmoid(from_msg[:, reset] + from_state[:, reset] + bias[:, reset])
    candidate = jnp.tanh(from_msg[:, last] + bias[:, last] + reset_gate * from_state[:, last])
    updated = (1.0 - update_gate) * candidate + update_gate * memory[...]
    new_memory[...] = jnp.where(count > 0, updated, memory[...])


def local(
    memory,
    want_end,
    want_near,
    end_slot,
    near_slot,
    near_count,
    event_time,
    near_time,
    frequency,
    phases,
    query_weight,
    key_weight,
    value_weight,
    out_weight,
    out_bias,
    message_in,
    message_out,
    input_weight,
    state_weight,
    update_bias,
):
    groups = lax.axis_size("grp")
    members = lax.axis_size("dev")
    nodes, row_width = memory.shape
    events = end_slot.shape[0]
    block = groups * CAP_N
    ends = groups * CAP_E
    places = block + ends
    mem_half = lax.optimization_barrier(memory.astype(jnp.bfloat16))
    counted = jnp.transpose(near_count)

    near_value = jnp.transpose(near_slot)
    end_value = jnp.transpose(end_slot)
    first, rank_or_none = pl.pallas_call(
        request_kernel,
        out_shape=(
            jax.ShapeDtypeStruct((groups, LANES), jnp.int32),
            jax.ShapeDtypeStruct((members, places), jnp.int32),
        ),
        in_specs=[pl.BlockSpec(memory_space=pltpu.SMEM)]
        + [pl.BlockSpec(memory_space=pltpu.VMEM)] * 5,
        name="request_kernel",
    )(
        lax.axis_index("dev").reshape(1),
        near_value,
        end_value,
        counted,
        jnp.transpose(want_end.reshape(-1, CAP_E)),
        jnp.transpose(want_near.reshape(-1, CAP_N)),
    )
    first = exchange(first, "grp")

    near_value = near_value.reshape(-1)
    end_value = end_value.reshape(-1)
    near_member, near_place = split_slot(near_value, members, CAP_N)
    end_member, end_place = split_slot(end_value, members, CAP_E)
    usable = (jnp.arange(K)[None, :, None] < counted[:, None, :]).reshape(-1)
    member = jnp.concatenate([jnp.where(usable, near_member, -1), end_member])
    place = jnp.concatenate([near_place, end_place + block])
    listed = jnp.sum(
        jnp.where(
            rank_or_none[:, None, :] == jnp.arange(CAP)[None, :, None],
            jnp.arange(places)[None, None, :],
            0,
        ),
        axis=2,
    )
    ref_rank = jnp.sum(
        jnp.dot(
            jnp.minimum(rank_or_none, CAP).astype(jnp.bfloat16),
            hot(place, places, 0),
            preferred_element_type=jnp.float32,
        )
        * hot(member, members, 0).astype(jnp.float32),
        axis=0,
    ).astype(jnp.int32)
    index = jnp.where(member >= 0, member * CAP + jnp.minimum(ref_rank, CAP - 1), 0)

    got_near = first[:, members * CAP_E : members * CAP_E + CAP_N]
    most = jnp.max(first[:, members * CAP_E + CAP_N :])
    passed = jnp.transpose(
        first[:, : members * CAP_E].reshape(groups, CAP_E, members), (2, 0, 1)
    ).reshape(members, ends)
    second = jnp.concatenate(
        [passed, listed, jnp.zeros((members, LANES - ends - CAP), jnp.int32)], 1
    )
    second = jnp.where(jnp.arange(LANES)[None, :] < ends + CAP, second, most)
    second = exchange(second, "dev")
    got_listed = second[:, ends : ends + CAP]
    most = jnp.max(second[:, ends + CAP :])
    got_code = second[:, :ends].reshape(members, groups, CAP_E)
    got_code = jnp.transpose(got_code, (1, 0, 2)).reshape(groups, members * CAP_E)
    got_end = jnp.where(got_code >= 0, got_code & (SHIFT - 1), -1)
    got_count = jnp.where(got_code >= 0, got_code >> 16, 0)

    row_index = jnp.concatenate([got_near, got_end], 1).reshape(-1)
    rows = exchange(pick(row_index, mem_half).reshape(groups, -1, row_width), "grp")
    near_block = rows[:, :CAP_N].reshape(block, row_width)
    end_part = jnp.transpose(
        rows[:, CAP_N:].reshape(groups, members, CAP_E, row_width), (1, 0, 2, 3)
    ).reshape(members, ends, row_width)
    near_part = pick(got_listed.reshape(-1), near_block).reshape(members, CAP, row_width)
    listed_ends = jnp.einsum(
        "dcp,dpw->dcw",
        hot(got_listed - block, ends, 2),
        end_part,
        preferred_element_type=jnp.float32,
    )
    table = exchange(near_part + listed_ends.astype(jnp.bfloat16), "dev")
    table = table.reshape(members * CAP, row_width)

    elapsed = (event_time[None, :] - jnp.transpose(near_time)).astype(jnp.float32)
    elapsed = elapsed.reshape(2, K, events)

    def by_owner(sums):
        return sums.reshape(groups * members, CAP_E, row_width)

    def whole():
        full = jnp.broadcast_to(near_block[None], (members, block, row_width))
        full = exchange(jnp.concatenate([full, end_part], 1), "dev")
        fetched = jnp.take(
            full.reshape(members * places, row_width),
            jnp.where(member >= 0, member * places + place, 0),
            axis=0,
            mode="clip",
        )
        embedded, message = event_block(
            fetched[2 * K * events :].reshape(2, events, row_width),
            fetched[: 2 * K * events].reshape(2, K, events, row_width),
            elapsed,
            counted,
            frequency,
            phases,
            query_weight,
            key_weight,
            value_weight,
            out_weight,
            out_bias,
            message_in,
            message_out,
        )
        message = message.reshape(-1, row_width)
        high = lax.reduce_precision(message, 8, 7)
        end_hot = hot(end_value, groups * members * CAP_E, 0)
        slot_sum = jnp.dot(
            end_hot, high.astype(jnp.bfloat16), preferred_element_type=jnp.float32
        ) + jnp.dot(
            end_hot, (message - high).astype(jnp.bfloat16), preferred_element_type=jnp.float32
        )
        return jnp.concatenate([embedded[0], embedded[1]], 1), by_owner(slot_sum.astype(jnp.bfloat16))

    pairs = 2 * events
    near_lanes = jnp.transpose(index[: 2 * K * events].reshape(2, K, events), (1, 0, 2))
    lanes = jnp.concatenate([near_lanes.reshape(-1), index[2 * K * events :]])
    elapsed_lanes = jnp.transpose(elapsed, (1, 0, 2)).reshape(K, 1, pairs)
    code = jnp.cos(elapsed_lanes * frequency[None, :, None] + phases[None, :, None])
    fixed = jnp.cos(phases)[None, :]
    operands = (
        counted.reshape(1, pairs),
        end_value.reshape(1, pairs),
        code.astype(jnp.bfloat16),
        fixed.astype(jnp.bfloat16),
        jnp.transpose(query_weight),
        jnp.transpose(jnp.concatenate([key_weight, value_weight], 1)),
        jnp.transpose(out_weight),
        out_bias[None, :],
        jnp.transpose(message_in),
        jnp.transpose(message_out),
    )

    def listed_only():
        embedded, slot_sum = pl.pallas_call(
            event_kernel,
            out_shape=(
                jax.ShapeDtypeStruct((events, 2 * row_width), jnp.bfloat16),
                jax.ShapeDtypeStruct((groups * members * CAP_E, row_width), jnp.bfloat16),
            ),
            in_specs=[pl.BlockSpec(memory_space=pltpu.SMEM)]
            + [pl.BlockSpec(memory_space=pltpu.VMEM)] * (1 + len(operands)),
            scratch_shapes=[pltpu.VMEM((row_width // LANES, table.shape[0], LANES), jnp.float32)]
            + [pltpu.VMEM((pairs, LANES), jnp.float32)] * 4
            + [
                pltpu.VMEM((K, row_width, pairs), jnp.float32),
                pltpu.VMEM((K, 8, pairs), jnp.float32),
            ],
            name="event_kernel",
        )(lanes, table, *operands)
        return embedded, by_owner(slot_sum)

    embedded, slot_sum = lax.cond(most > CAP, whole, listed_only)
    news = exchange(
        slot_sum, ("grp", "dev")
    ).reshape(-1, row_width)
    owned = got_end.reshape(-1)
    step = 128
    new_memory = pl.pallas_call(
        gru_kernel,
        grid=(nodes // step,),
        out_shape=jax.ShapeDtypeStruct(memory.shape, memory.dtype),
        in_specs=[
            pl.BlockSpec(news.shape, lambda i: (0, 0)),
            pl.BlockSpec((1, owned.shape[0]), lambda i: (0, 0)),
            pl.BlockSpec((1, owned.shape[0]), lambda i: (0, 0)),
            pl.BlockSpec((step, row_width), lambda i: (i, 0)),
            pl.BlockSpec((step, 3 * row_width), lambda i: (i, 0)),
            pl.BlockSpec(input_weight.shape, lambda i: (0, 0)),
            pl.BlockSpec((1, 3 * row_width), lambda i: (0, 0)),
        ],
        out_specs=pl.BlockSpec((step, row_width), lambda i: (i, 0)),
        name="gru_kernel",
    )(
        news,
        owned[None, :],
        got_count.reshape(1, -1),
        memory,
        jnp.dot(mem_half, state_weight, preferred_element_type=jnp.float32),
        input_weight,
        update_bias[None, :],
    )
    return (new_memory, embedded)


def solution(mesh):
    in_specs = (
        P(("grp", "dev"), None),
        P(("grp", "dev"), None, None),
        P(("grp", "dev"), None, None),
        P(("grp", "dev"), None),
        P(("grp", "dev"), None),
        P(("grp", "dev"), None),
        P(("grp", "dev")),
        P(("grp", "dev"), None),
        P(),
        P(),
        P(),
        P(),
        P(),
        P(),
        P(),
        P(),
        P(),
        P(),
        P(),
        P(),
    )
    out_specs = (P(("grp", "dev"), None), P(("grp", "dev"), None))
    return jax.shard_map(local, mesh=mesh, in_specs=in_specs, out_specs=out_specs, check_vma=False)
```
